512 devices in a mesh: seq: 128 (over y, x_hi, z), coal: 4 (over x_lo, core).
Axes of the slice: x: 4 (x_hi: 2, x_lo: 2; x = x_hi * 2 + x_lo), y: 4, z: 16, core: 2. Of those that a mesh axis runs over, the one named last changes fastest.
Arguments:
- lat_q: bfloat16 [1024, 1536], P('seq'), may hold values from -4.5 to 4.5
- lat_k: bfloat16 [1024, 1536], P('seq'), may hold values from -4.5 to 4.5
- lat_v: bfloat16 [1024, 1536], P('seq'), may hold values from -6 to 6
- txt_q: bfloat16 [512, 1536], P('seq'), may hold values from -4.5 to 4.5
- txt_k: bfloat16 [512, 1536], P('seq'), may hold values from -4.5 to 4.5
- txt_v: bfloat16 [512, 1536], P('seq'), may hold values from -6 to 6
- span_ids: int32 [512], P('seq'), may hold values from 0 to 15, never falling along the last dimension, each value on 1 to 128 neighbouring positions
- coal_bits: int32 [32], P('coal'), may hold values from 0 to 65535
Outputs:
- txt_out: bfloat16 [32, 512, 1536], P('coal', 'seq')
- lat_out: bfloat16 [32, 1024, 1536], P('coal', 'seq')
The draws below stay inside these ranges and needn't reach their ends.
Inputs may be any that keep to these rules, and one draw needn't show every extreme that they name: `span_ids`: span ids never fall along the text tokens; each of the 16 spans has one token or more, and the longest has 128.
All inputs are finite; a program needn't handle non-finite values.
Results may differ from the reference program's by a relative error of at most 0.0049.
Values may be sent and summed in bfloat16 or wider, within the bound.
A program may use at most 64 MiB of HBM per device.

```python
import math
import jax
import jax.numpy as jnp
import numpy as np
from jax import lax

HEADS = 12
HD = 128
SPANS = 16
LAT = 1024
TXT = 512
COALS = 32


def base_values(key, row_count, columns):
    return 1.7 * jax.random.truncated_normal(key, -2.6, 2.6, (row_count, columns), jnp.float32)


def draw_lat_q(key, part):
    columns = HEADS * HD
    values_drawn = base_values(jax.random.fold_in(key, 1), LAT, columns)
    return values_drawn.astype(jnp.bfloat16)


def draw_lat_k(key, part):
    columns = HEADS * HD
    values_drawn = base_values(jax.random.fold_in(key, 2), LAT, columns)
    return values_drawn.astype(jnp.bfloat16)


def set_ends(entries, own_key, low, high):
    spot = [jax.random.randint(jax.random.fold_in(own_key, axis), (), 0, length) for axis, length in enumerate(entries.shape)]
    longest = entries.shape.index(max(entries.shape))
    next_to = spot[:longest] + [(spot[longest] + 1) % entries.shape[longest]] + spot[longest + 1:]
    return entries.at[tuple(spot)].set(low).at[tuple(next_to)].set(high)


def level_of(stream_key, shape, pieces, smallest, largest):
    gain, own = 1.0, jax.random.fold_in(stream_key, 6)
    for dim, shards_of in pieces:
        heights = jnp.exp(jax.random.uniform(jax.random.fold_in(own, dim), (shards_of,), jnp.float32, smallest / len(pieces), largest / len(pieces)))
        gain = gain * jnp.repeat(heights, shape[dim] // shards_of).reshape([-1 if axis == dim else 1 for axis in range(len(shape))])
    return gain


def length_profile(count, total, bound, skew):
    loads = [(1 << 20) // math.isqrt(grade ** skew) + 1 for grade in range(2, count + 1)]
    surplus, holding = total - bound - (count - 1), [1] * (count - 1)
    while surplus > 0:
        candidates = [i for i in range(count - 1) if holding[i] < bound]
        pool, left = sum([loads[i] for i in candidates]), surplus
        for i in candidates:
            more = min(bound - holding[i], max(1, left * loads[i] // pool), surplus)
            holding[i] = holding[i] + more
            surplus = surplus - more
    return np.array([bound] + holding)


def ragged(own_key, count, total, bound, skew):
    if count == 2:
        one = jax.random.randint(own_key, (), max(1, total - bound), min(bound, total - 1) + 1)
        return jnp.stack([one, total - one])
    lengths = jnp.asarray(length_profile(count, total, bound, skew), jnp.int32)
    twos = (count - 1) // 2
    donor, receiver = lengths[1:1 + 2 * twos:2], lengths[2:2 + 2 * twos:2]
    slack = jnp.minimum(donor - 1, bound - receiver)
    moved = jax.random.randint(jax.random.fold_in(own_key, 1), (twos,), 0, 1 << 20) % (slack + 1)
    lengths = lengths.at[1:1 + 2 * twos:2].set(donor - moved).at[2:2 + 2 * twos:2].set(receiver + moved)
    return lengths[jax.random.permutation(jax.random.fold_in(own_key, 2), count)]


def normal_values(key, shape, width, reach, pieces=(), held_as=jnp.bfloat16):
    gain = level_of(key, shape, pieces, -0.22, 0.18) if pieces else 1.0
    drawn = jax.random.normal(key, shape, jnp.float32) * width * gain
    return jnp.minimum(jnp.maximum(drawn, -reach), reach).astype(held_as)


def setup_inputs(seed: int = 0) -> dict:
    arg_keys = jax.random.split(jax.random.key(seed), 9)
    lat_q = draw_lat_q(jax.random.fold_in(arg_keys[8], 71), 0)
    lat_k = draw_lat_k(jax.random.fold_in(arg_keys[8], 71), 0)
    lat_v = normal_values(arg_keys[2], (LAT, HEADS * HD), 1.0, 6.0, ((0, 128),))
    txt_q = normal_values(arg_keys[3], (TXT, HEADS * HD), 1.7, 4.5, ((0, 128),))
    txt_k = normal_values(arg_keys[4], (TXT, HEADS * HD), 1.7, 4.5, ((0, 128),))
    txt_v = normal_values(arg_keys[5], (TXT, HEADS * HD), 1.0, 6.0, ((0, 128),))
    span_ids = jnp.searchsorted(jnp.cumsum(ragged(arg_keys[6], SPANS, TXT, TXT // 4, 2)), jnp.arange(TXT), side="right").astype(jnp.int32)
    coal_bits = set_ends(jax.random.randint(arg_keys[7], (COALS,), 0, 2 ** SPANS), jax.random.fold_in(arg_keys[7], 1), 0, (2 ** SPANS) - 1).astype(jnp.int32)
    return dict(lat_q=lat_q, lat_k=lat_k, lat_v=lat_v, txt_q=txt_q, txt_k=txt_k, txt_v=txt_v, span_ids=span_ids, coal_bits=coal_bits)


def reference(lat_q, lat_k, lat_v, txt_q, txt_k, txt_v, span_ids, coal_bits):
    queries = jnp.concatenate([txt_q, lat_q], axis=0)
    key_rows = jnp.concatenate([txt_k, lat_k], axis=0)
    value_rows = jnp.concatenate([txt_v, lat_v], axis=0)
    total_rows = queries.shape[0]
    allowed_text = jnp.right_shift(coal_bits[:, None], span_ids[None, :]) & 1 == 1
    allowed = jnp.concatenate([allowed_text, jnp.ones((COALS, LAT), dtype=jnp.bool_)], axis=1)
    scaling = 1.0 / math.sqrt(HD)

    def by_head(tensor):
        return jnp.transpose(tensor.reshape(total_rows, HEADS, HD), (1, 0, 2))

    def one_head(operands):
        head_q, head_k, head_v = operands
        scores = jnp.dot(head_q, head_k.T, preferred_element_type=jnp.float32) * scaling

        def one_coalition(visible):
            masked = jnp.where(visible[None, :], scores, -jnp.inf)
            maxima = lax.optimization_barrier(jnp.max(masked, axis=1, keepdims=True))
            weights = jnp.exp(masked - maxima)
            totals = lax.optimization_barrier(jnp.sum(weights, axis=1, keepdims=True))
            mixed = jnp.dot(weights.astype(jnp.bfloat16), head_v, preferred_element_type=jnp.float32)
            return mixed / totals
        return lax.map(one_coalition, allowed)
    outputs = lax.map(one_head, (by_head(queries), by_head(key_rows), by_head(value_rows)))
    merged = jnp.transpose(outputs, (1, 2, 0, 3)).reshape(COALS, total_rows, HEADS * HD).astype(jnp.bfloat16)
    return (merged[:, :TXT], merged[:, TXT:])
```

```python
import functools
import math

import jax
import jax.numpy as jnp
from jax import lax
from jax.experimental import pallas as pl
from jax.experimental.pallas import tpu as pltpu
from jax.sharding import PartitionSpec as P

MESH = pl.DeviceIdType.MESH
BF16, F32 = jnp.bfloat16, jnp.float32

YS, XS, ZS = 4, 4, 16
ROWS_Y = 3
HD = 128
SCALE2 = math.log2(math.e) / math.sqrt(HD)
HIDDEN = -1e30
UNITS = 13
FAR = 5


def place():
    seq, coal = lax.axis_index("seq"), lax.axis_index("coal")
    return lax.div(seq, 32), lax.rem(lax.div(seq, 16), 2), lax.rem(seq, 16), lax.div(coal, 2), lax.rem(coal, 2)


def device(y, x, z, core):
    return ((y * 2 + lax.div(x, 2)) * ZS + z, lax.rem(x, 2) * 2 + core)


def widened(unit):
    return unit.astype(F32)


def kernel(
    spans, bits, lq, lk, lv, tq, tk, tv, out_t, out_l,
    own, queries, biases, gathered, text_k, text_v, lat_k, lat_v, bias_rows, base_q, lat_stats, lat_mixed, results, landed,
    s0_send, s0_recv, q0_send, q0_recv, b_send, b_recv, z_send, z_recv, c_send, c_recv, o_send, o_recv,
):
    y, x_hi, z, x_lo, core = place()
    x = x_hi * 2 + x_lo
    coal = x_lo * 2 + core
    active = y < ROWS_Y

    def at_z(shift):
        return device(y, x, lax.rem(z + shift + ZS, ZS), core)

    barrier = pltpu.get_barrier_semaphore()
    partners = []
    for dy in range(YS):
        for dx in range(XS):
            for dc in range(2):
                if dy or dx or dc:
                    partners.append(
                        device(lax.rem(y + dy, YS), lax.rem(x + dx, XS), z, lax.rem(core + dc, 2))
                    )
    for shift in (1, 2, 3, FAR):
        partners.append(at_z(shift))
        partners.append(at_z(-shift))
    for partner in partners:
        pl.semaphore_signal(barrier, inc=1, device_id=partner, device_id_type=MESH)

    sub = lax.broadcasted_iota(jnp.int32, (8, HD), 0)
    lane = lax.broadcasted_iota(jnp.int32, (8, HD), 1)
    upper = sub < 4
    x_to = jnp.where(core == 0, x, jnp.where(x_lo == 0, lax.rem(x + 3, XS), lax.rem(x + 1, XS)))
    span = jnp.zeros((8, HD), jnp.int32)
    for row in range(4):
        span = jnp.where(sub == 4 + row, spans[row], span)
    one_hot = jnp.where((lane == span + 16 * lax.div(y, 2)), 1.0, 0.0)
    for y_to in range(ROWS_Y):
        cols = pl.ds(pl.multiple_of((x_to * ROWS_Y + y_to) * HD, HD), HD)
        own[y_to, 0] = jnp.concatenate([widened(tk[:, cols]), widened(tv[:, cols])], axis=0).astype(BF16)
        own[y_to, 1] = lk[:, cols]
        own[y_to, 2] = lv[:, cols]
        asked = widened(tq[:, cols])
        own[y_to, 3] = jnp.where(upper, jnp.concatenate([asked, asked], axis=0), one_hot).astype(BF16)
        own[y_to, 4] = lq[:, cols]
    kept = jnp.zeros((8, HD), jnp.int32)
    for row in range(8):
        kept = jnp.where(sub == row, bits[row], kept)
    shown = jnp.right_shift(kept, jnp.bitwise_and(lane, 15)) & 1
    biases[coal] = jnp.where((lane < 32) & (shown == 0), HIDDEN, 0.0).astype(BF16)
    text_v[:, HD:] = jnp.ones((512, HD), BF16)
    lat_v[:, HD:] = jnp.ones((1024, HD), BF16)

    pl.semaphore_wait(barrier, len(partners))

    def rows_to(y_to):
        target = device(jnp.int32(y_to), x_to, z, x_hi)
        return [
            (own.at[y_to, pl.ds(0, 3)], gathered.at[0, x_hi, pl.ds(y * 3, 3)], s0_send.at[y_to], s0_recv.at[y], target),
            (own.at[y_to, pl.ds(3, 2)], queries.at[y], q0_send.at[y_to], q0_recv.at[y], target),
        ]

    def remote(src, dst, send, recv, target):
        return pltpu.make_async_remote_copy(
            src_ref=src, dst_ref=dst, send_sem=send, recv_sem=recv, device_id=target, device_id_type=MESH
        )

    for y_to in range(ROWS_Y):
        to_self = (core == 0) & (x_hi == 0) & (y == y_to)
        for src, dst, send, recv, target in rows_to(y_to):

            @pl.when(to_self)
            def _():
                pltpu.make_async_copy(src, dst, recv).start()

            @pl.when(jnp.logical_not(to_self))
            def _():
                remote(src, dst, send, recv, target).start()

    def bias_copies():
        chip = x_hi * 2 + 1 - x_lo
        for n, target in enumerate((device(y, x, z, 1 - core), device(y, chip, z, core), device(y, chip, z, 1 - core))):
            yield remote(biases.at[coal], biases.at[coal], b_send.at[n], b_recv.at[coal], target)

    def ring(offset, shift, n, first=0, count=UNITS):
        here = gathered.at[offset % ZS, core, pl.ds(first, count)]
        there = gathered.at[(offset - shift) % ZS, core, pl.ds(first, count)]
        return remote(here, there, z_send.at[n], z_recv.at[n], at_z(shift))

    def across(offset):
        block = gathered.at[offset % ZS, core]
        return remote(block, block, c_send.at[offset % ZS], c_recv.at[offset % ZS], device(y, x, z, 1 - core))

    half = UNITS // 2
    stage_one = [(0, FAR), (0, -FAR), (0, 1), (0, -1), (0, 2), (0, -2)]
    stage_two = [
        (FAR, -3, half, UNITS - half), (-FAR, 3, 0, half),
        (FAR, 1), (FAR, -1), (-FAR, 1), (-FAR, -1), (FAR, 2), (FAR, -2), (-FAR, 2), (-FAR, -2),
    ]

    def stage_one_copies():
        return [ring(o, s, n) for n, (o, s) in enumerate(stage_one)]

    def stage_two_copies():
        return [ring(c[0], c[1], len(stage_one) + n, *c[2:]) for n, c in enumerate(stage_two)]

    def converted(o):
        for k in range(2):
            part = [widened(gathered[o, k, n]) for n in range(UNITS)]
            keys, values = [], []
            for pair in range(2):
                one, two = part[pair * 6], part[pair * 6 + 3]
                keys.append(jnp.where(upper, one, pltpu.roll(two, 4, 0)))
                values.append(jnp.where(upper, pltpu.roll(one, 4, 0), two))
            marks = [jnp.where(lane < 16, part[12], 0.0), jnp.where(lane < 16, 0.0, part[12])]
            rows = pl.ds((o * 2 + k) * 16, 16)
            text_k[rows, pl.ds(0, HD)] = jnp.concatenate(keys, axis=0).astype(BF16)
            text_k[rows, pl.ds(HD, HD)] = jnp.concatenate(marks, axis=0).astype(BF16)
            text_v[rows, pl.ds(0, HD)] = jnp.concatenate(values, axis=0).astype(BF16)
            rows = pl.ds((o * 2 + k) * 32, 32)
            lat_k[rows, :] = jnp.concatenate([part[n * 3 + 1] for n in range(4)], axis=0).astype(BF16)
            lat_v[rows, pl.ds(0, HD)] = jnp.concatenate([part[n * 3 + 2] for n in range(4)], axis=0).astype(BF16)

    nt = (((1,), (1,)), ((), ()))

    @pl.when(active)
    def _():
        for copy in bias_copies():
            copy.start()
        for n in range(YS):
            pltpu.make_async_copy(queries.at[n], queries.at[n], q0_recv.at[n]).wait()
        units = [widened(queries[n, 0]) for n in range(YS)]
        marks = [jnp.where(upper, pltpu.roll(units[n], 4, 0), units[n + 1]) for n in (0, 2)]
        own_marks = jnp.where(lane < 16, marks[0], marks[1])
        gathered[0, core, 12] = own_marks.astype(BF16)
        for n in range(YS):
            block = gathered.at[0, core, pl.ds(n * 3, 3)]
            pltpu.make_async_copy(block, block, s0_recv.at[n]).wait()
        first = stage_one_copies()
        for copy in first:
            copy.start()
        crossing = [across(o) for o in range(ZS)]
        crossing[0].start()

        for n in range(YS):
            twice = jnp.where(upper, units[n], pltpu.roll(units[n], 4, 0))
            base_q[pl.ds(n * 16, 16), :] = jnp.concatenate([twice, widened(queries[n, 1])], axis=0).astype(BF16)

        second = stage_two_copies()
        for n, fast in ((0, (1, 6, 7, 8, 9)), (1, (0, 2, 3, 4, 5))):
            first[n].wait_recv()
        for copy in second:
            copy.start()
        crossing[FAR].start()
        crossing[ZS - FAR].start()
        for n in range(2, 6):
            first[n].wait_recv()
            crossing[-stage_one[n][1] % ZS].start()
        for g in range(4):

            @pl.when(coal != g)
            def _():
                pltpu.make_async_copy(biases.at[g], biases.at[g], b_recv.at[g]).wait()

            unit = widened(biases[g])
            rows = [unit[c : c + 1, :] for c in range(8)]
            parts = [jnp.where(upper, rows[2 * p], rows[2 * p + 1]) for p in range(4)]
            parts += [jnp.broadcast_to(row, (8, HD)) for row in rows]
            bias_rows[g] = jnp.concatenate(parts, axis=0).astype(BF16)
        second[0].wait_recv()
        second[1].wait_recv()
        crossing[8].start()
        for n in range(2, 10):
            second[n].wait_recv()
            crossing[(stage_two[n][0] - stage_two[n][1]) % ZS].start()
        for o in range(ZS):
            crossing[o].wait_recv()
            converted(o)

        scores = lax.dot_general(base_q[...], lat_k[...], nt, preferred_element_type=F32) * SCALE2
        maxima = jnp.max(scores, axis=1, keepdims=True)
        weights = jnp.exp2(scores - maxima).astype(BF16)
        lat_stats[...] = jnp.broadcast_to(maxima, (64, HD))
        lat_mixed[...] = jnp.dot(weights, lat_v[...], preferred_element_type=F32)

        head = x * ROWS_Y + y

        def to_device(step):
            row, g = lax.div(step, 4), lax.rem(step, 4)
            target = (((row * 2 + core) * ZS + z), g)
            return (
                (row == y) & (core == x_hi) & (g == coal),
                remote(results.at[step], landed.at[head], o_send.at[step], o_recv.at[head], target),
            )

        def spread(text, latent):
            return jnp.concatenate([text] * 4 + [latent] * 8, axis=0)

        def one_device(step, _):
            row, g = lax.div(step, 4), lax.rem(step, 4)
            at_text = pl.ds(pl.multiple_of(row * 16, 16), 8)
            at_latent = pl.ds(pl.multiple_of(row * 16 + 8, 8), 8)
            asked = base_q[pl.ds(pl.multiple_of(row * 16, 16), 16), :].astype(F32)
            left = spread(asked[:8], asked[8:]).astype(BF16)
            full = jnp.concatenate([left, bias_rows[g]], axis=1)
            scores = lax.dot_general(full, text_k[...], nt, preferred_element_type=F32) * SCALE2
            shared = spread(lat_stats[at_text, :], lat_stats[at_latent, :])[:, :1]
            maxima = jnp.maximum(jnp.max(scores, axis=1, keepdims=True), shared)
            weights = jnp.exp2(scores - maxima).astype(BF16)
            total = jnp.dot(weights, text_v[...], preferred_element_type=F32)
            total = total + jnp.exp2(shared - maxima) * spread(lat_mixed[at_text, :], lat_mixed[at_latent, :])
            results[step] = (total[:, :HD] / total[:, HD:]).astype(BF16)
            to_self, copy = to_device(step)

            @pl.when(to_self)
            def _():
                pltpu.make_async_copy(results.at[step], landed.at[head], o_recv.at[head]).start()

            @pl.when(jnp.logical_not(to_self))
            def _():
                copy.start()

            return 0

        lax.fori_loop(0, 16, one_device, 0)

        for copy in first + second:
            copy.wait_send()
        for copy in crossing:
            copy.wait_send()
        for copy in bias_copies():
            copy.wait_send()

        def drained(step, _):
            to_self, copy = to_device(step)

            @pl.when(jnp.logical_not(to_self))
            def _():
                copy.wait_send()

            return 0

        lax.fori_loop(0, 16, drained, 0)

    for y_to in range(ROWS_Y):
        to_self = (core == 0) & (x_hi == 0) & (y == y_to)
        for src, dst, send, recv, target in rows_to(y_to):

            @pl.when(jnp.logical_not(to_self))
            def _():
                remote(src, dst, send, recv, target).wait_send()

    for head in range(ROWS_Y * XS):
        pltpu.make_async_copy(landed.at[head], landed.at[head], o_recv.at[head]).wait()
        out_t[:, head * HD : (head + 1) * HD] = landed[head, :32]
        out_l[:, head * HD : (head + 1) * HD] = landed[head, 32:]


def per_device(lat_q, lat_k, lat_v, txt_q, txt_k, txt_v, span_ids, coal_bits):
    vmem = pl.BlockSpec(memory_space=pltpu.VMEM)
    smem = pl.BlockSpec(memory_space=pltpu.SMEM)
    dma = pltpu.SemaphoreType.DMA
    out_t, out_l = pl.pallas_call(
        kernel,
        out_shape=(jax.ShapeDtypeStruct((32, 1536), BF16), jax.ShapeDtypeStruct((64, 1536), BF16)),
        in_specs=[smem, smem] + [vmem] * 6,
        out_specs=(vmem, vmem),
        scratch_shapes=[
            pltpu.VMEM((ROWS_Y, 5, 8, HD), BF16),
            pltpu.VMEM((YS, 2, 8, HD), BF16),
            pltpu.VMEM((4, 8, HD), BF16),
            pltpu.VMEM((ZS, 2, UNITS, 8, HD), BF16),
            pltpu.VMEM((512, 2 * HD), BF16),
            pltpu.VMEM((512, 2 * HD), BF16),
            pltpu.VMEM((1024, HD), BF16),
            pltpu.VMEM((1024, 2 * HD), BF16),
            pltpu.VMEM((4, 96, HD), BF16),
            pltpu.VMEM((64, HD), BF16),
            pltpu.VMEM((64, HD), F32),
            pltpu.VMEM((64, 2 * HD), F32),
            pltpu.VMEM((16, 96, HD), BF16),
            pltpu.VMEM((12, 96, HD), BF16),
            dma((3,)), dma((4,)), dma((3,)), dma((4,)), dma((3,)), dma((4,)),
            dma((16,)), dma((16,)), dma((16,)), dma((16,)), dma((16,)), dma((12,)),
        ],
        compiler_params=pltpu.CompilerParams(collective_id=0, has_side_effects=True),
        name="coalition_attention",
    )(span_ids, coal_bits, lat_q, lat_k, lat_v, txt_q, txt_k, txt_v)
    return out_t.reshape(8, 4, 1536), out_l.reshape(8, 8, 1536)


def solution(mesh):
    return jax.shard_map(
        per_device,
        mesh=mesh,
        in_specs=(P("seq", None),) * 6 + (P("seq"), P("coal")),
        out_specs=(P("coal", "seq", None), P("coal", "seq", None)),
        check_vma=False,
    )
```

```python
import functools
import math

import jax
import jax.numpy as jnp
from jax import lax
from jax.experimental import pallas as pl
from jax.experimental.pallas import tpu as pltpu
from jax.sharding import PartitionSpec as P

MESH = pl.DeviceIdType.MESH
BF16, F32 = jnp.bfloat16, jnp.float32

YS, XS, ZS = 4, 4, 16
ROWS_Y = 3
HD = 128
SCALE2 = math.log2(math.e) / math.sqrt(HD)
HIDDEN = -1e30
PARTS = 7
FAR = 5
SHIFTS = (FAR, -FAR, 2, -2, 1, -1, 0)


def place():
    seq, coal = lax.axis_index("seq"), lax.axis_index("coal")
    return lax.div(seq, 32), lax.rem(lax.div(seq, 16), 2), lax.rem(seq, 16), lax.div(coal, 2), lax.rem(coal, 2)


def device(y, x, z, core):
    return ((y * 2 + lax.div(x, 2)) * ZS + z, lax.rem(x, 2) * 2 + core)


def widened(unit):
    return unit.astype(F32)


def kernel(
    spans_in, bits_in, lq_in, lk_in, lv_in, tq_in, tk_in, tv_in, landed,
    spans, bits, lq, lk, lv, tq, tk, tv,
    own, own_q, queries, biases, gathered, text_k, text_v, lat_k, lat_v, bias_rows, base_q, lat_stats, lat_mixed, results,
    in_sem, s_send, s_recv, q_send, q_recv, b_send, b_recv, z_send, z_recv, c_send, c_recv, o_send, o_recv,
):
    y, x_hi, z, x_lo, core = place()
    x = x_hi * 2 + x_lo
    coal = x_lo * 2 + core
    active = y < ROWS_Y

    def at_z(shift):
        return device(y, x, lax.rem(z + shift + ZS, ZS), core)

    loads = [
        pltpu.make_async_copy(src, dst, in_sem.at[n])
        for n, (src, dst) in enumerate(
            ((spans_in, spans), (bits_in, bits), (tk_in, tk), (tv_in, tv), (lk_in, lk), (lv_in, lv), (tq_in, tq), (lq_in, lq))
        )
    ]
    for load in loads:
        load.start()

    barrier = pltpu.get_barrier_semaphore()

    def greet(partner):
        pl.semaphore_signal(barrier, inc=1, device_id=partner, device_id_type=MESH)

    x_from = jnp.where(core == x_hi, x, jnp.where(x_lo == 0, lax.rem(x + 3, XS), lax.rem(x + 1, XS)))
    core_from = jnp.where(core == x_hi, 0, 1)
    other_chip = x_hi * 2 + 1 - x_lo
    others = (device(y, x, z, 1 - core), device(y, other_chip, z, core), device(y, other_chip, z, 1 - core))

    @pl.when(active)
    def _():
        for shift in SHIFTS:
            for y_from in range(YS):
                source = device(jnp.int32(y_from), x_from, lax.rem(z - shift + ZS, ZS), core_from)
                if shift:
                    greet(source)
                else:

                    @pl.when(jnp.logical_not((y == y_from) & (core == x_hi) & (core == 0)))
                    def _():
                        greet(source)

        for shift in (1, 2, 3):
            greet(at_z(shift))
            greet(at_z(-shift))
        for other in others:
            greet(other)

    for y_from in range(ROWS_Y):
        for x_of in range(XS):

            @pl.when(jnp.logical_not((y == y_from) & (x == x_of) & (core == x_hi)))
            def _():
                greet(device(jnp.int32(y_from), jnp.int32(x_of), z, x_hi))

    for load in loads:
        load.wait()

    sub = lax.broadcasted_iota(jnp.int32, (8, HD), 0)
    lane = lax.broadcasted_iota(jnp.int32, (8, HD), 1)
    upper = sub < 4
    x_to = jnp.where(core == 0, x, jnp.where(x_lo == 0, lax.rem(x + 3, XS), lax.rem(x + 1, XS)))
    span = jnp.zeros((8, HD), jnp.int32)
    for row in range(4):
        span = jnp.where(sub == row, spans[row], span)
    one_hot = jnp.where(lane == span, 1.0, 0.0)[:4]
    for y_to in range(ROWS_Y):
        cols = pl.ds(pl.multiple_of((x_to * ROWS_Y + y_to) * HD, HD), HD)
        keys, values, asked = widened(lk[:, cols]), widened(lv[:, cols]), widened(lq[:, cols])
        own[y_to, 0] = tk[:, cols]
        own[y_to, 1] = tv[:, cols]
        own[y_to, 2] = one_hot.astype(BF16)
        for n in range(2):
            own[y_to, 3 + n] = keys[n * 4 : n * 4 + 4].astype(BF16)
            own[y_to, 5 + n] = values[n * 4 : n * 4 + 4].astype(BF16)
            own_q[y_to, 1 + n] = asked[n * 4 : n * 4 + 4].astype(BF16)
        own_q[y_to, 0] = tq[:, cols]
    kept = jnp.zeros((8, HD), jnp.int32)
    for row in range(8):
        kept = jnp.where(sub == row, bits[row], kept)
    shown = jnp.right_shift(kept, jnp.bitwise_and(lane, 15)) & 1
    biases[coal] = jnp.where((lane < 16) & (shown == 0), HIDDEN, 0.0).astype(BF16)
    text_v[:, HD:] = jnp.ones((512, HD), BF16)
    lat_v[:, HD:] = jnp.ones((1024, HD), BF16)

    in_own = (core == 0) & (x_hi == 0) & active
    awaited = len(SHIFTS) * ROWS_Y - in_own.astype(jnp.int32)
    mine = 6 + 3 + 16 - (core == x_hi).astype(jnp.int32)
    pl.semaphore_wait(barrier, awaited + jnp.where(active, mine, 0))

    def remote(src, dst, send, recv, target):
        return pltpu.make_async_remote_copy(
            src_ref=src, dst_ref=dst, send_sem=send, recv_sem=recv, device_id=target, device_id_type=MESH
        )

    def rows_to(n, y_to):
        target = device(jnp.int32(y_to), x_to, lax.rem(z + SHIFTS[n] + ZS, ZS), x_hi)
        there = gathered.at[-SHIFTS[n] % ZS, x_hi, pl.ds(y * PARTS, PARTS)]
        return (own.at[y_to], there, s_send.at[n * ROWS_Y + y_to], s_recv.at[n * YS + y], target)

    def queries_to(y_to):
        target = device(jnp.int32(y_to), x_to, z, x_hi)
        return (own_q.at[y_to], queries.at[y], q_send.at[y_to], q_recv.at[y], target)

    def maybe_own(y_to, copy):
        src, dst, send, recv, target = copy
        to_self = in_own & (y == y_to)

        @pl.when(to_self)
        def _():
            pltpu.make_async_copy(src, dst, recv).start()

        @pl.when(jnp.logical_not(to_self))
        def _():
            remote(src, dst, send, recv, target).start()

    for n in range(len(SHIFTS)):
        for y_to in range(ROWS_Y):
            if SHIFTS[n]:
                remote(*rows_to(n, y_to)).start()
            else:
                maybe_own(y_to, rows_to(n, y_to))
                maybe_own(y_to, queries_to(y_to))

    def bias_copies():
        for n, target in enumerate(others):
            yield remote(biases.at[coal], biases.at[coal], b_send.at[n], b_recv.at[coal], target)

    whole = YS * PARTS

    def ring(n, offset, shift, first=0, count=whole):
        here = gathered.at[offset % ZS, core, pl.ds(first, count)]
        there = gathered.at[(offset - shift) % ZS, core, pl.ds(first, count)]
        return remote(here, there, z_send.at[n], z_recv.at[n], at_z(shift))

    def across(offset):
        block = gathered.at[offset % ZS, core]
        return remote(block, block, c_send.at[offset % ZS], c_recv.at[offset % ZS], others[0])

    half = whole // 2
    forwards = [
        (FAR, -3, half, whole - half), (-FAR, 3, 0, half),
        (FAR, 2), (FAR, -2), (FAR, 1), (FAR, -1), (-FAR, 2), (-FAR, -2), (-FAR, 1), (-FAR, -1),
    ]

    def direct_in(n):
        for y_from in range(YS):
            block = gathered.at[-SHIFTS[n] % ZS, core, pl.ds(y_from * PARTS, PARTS)]
            pltpu.make_async_copy(block, block, s_recv.at[n * YS + y_from]).wait()

    def converted(o):
        for k in range(2):
            part = [[widened(gathered[o, k, n * PARTS + m]) for m in range(PARTS)] for n in range(YS)]

            def rows_of(*which):
                return jnp.concatenate([part[n][m] for n in range(YS) for m in which], axis=0).astype(BF16)

            rows = pl.ds((o * 2 + k) * 16, 16)
            text_k[rows, pl.ds(0, HD)] = rows_of(0)
            text_k[rows, pl.ds(HD, HD)] = rows_of(2)
            text_v[rows, pl.ds(0, HD)] = rows_of(1)
            rows = pl.ds((o * 2 + k) * 32, 32)
            lat_k[rows, :] = rows_of(3, 4)
            lat_v[rows, pl.ds(0, HD)] = rows_of(5, 6)

    nt = (((1,), (1,)), ((), ()))

    @pl.when(active)
    def _():
        for copy in bias_copies():
            copy.start()
        second = [ring(n, *f) for n, f in enumerate(forwards)]
        crossing = [across(o) for o in range(ZS)]
        for n in (0, 1):
            direct_in(n)
            for f, copy in zip(forwards, second):
                if f[0] == -SHIFTS[n]:
                    copy.start()
            crossing[-SHIFTS[n] % ZS].start()
        for n in range(2, len(SHIFTS)):
            direct_in(n)
            crossing[-SHIFTS[n] % ZS].start()

        for n in range(YS):
            pltpu.make_async_copy(queries.at[n], queries.at[n], q_recv.at[n]).wait()
            asked = [widened(queries[n, m]) for m in (0, 0, 1, 2)]
            base_q[pl.ds(n * 16, 16), :] = jnp.concatenate(asked, axis=0).astype(BF16)
        for g in range(4):

            @pl.when(coal != g)
            def _():
                pltpu.make_async_copy(biases.at[g], biases.at[g], b_recv.at[g]).wait()

            unit = widened(biases[g])
            rows = [unit[c : c + 1, :] for c in range(8)]
            parts = [jnp.where(upper, rows[2 * p], rows[2 * p + 1]) for p in range(4)]
            parts += [jnp.broadcast_to(row, (8, HD)) for row in rows]
            bias_rows[pl.ds(g * 96, 96), :] = jnp.concatenate(parts, axis=0).astype(BF16)
        for shift in SHIFTS:
            crossing[-shift % ZS].wait_recv()
            converted(-shift % ZS)
        for n in range(2, len(forwards)):
            second[n].wait_recv()
            crossing[(forwards[n][0] - forwards[n][1]) % ZS].start()
        second[0].wait_recv()
        second[1].wait_recv()
        crossing[8].start()
        for n in list(range(2, len(forwards))) + [0]:
            o = (forwards[n][0] - forwards[n][1]) % ZS
            crossing[o].wait_recv()
            converted(o)

        scores = lax.dot_general(base_q[...], lat_k[...], nt, preferred_element_type=F32) * SCALE2
        maxima = jnp.max(scores, axis=1, keepdims=True)
        weights = jnp.exp2(scores - maxima).astype(BF16)
        lat_stats[...] = jnp.broadcast_to(maxima, (64, HD))
        lat_mixed[...] = jnp.dot(weights, lat_v[...], preferred_element_type=F32)

        head = x * ROWS_Y + y

        def to_device(row, g):
            target = (((row * 2 + core) * ZS + z), g)
            return (
                (row == y) & (core == x_hi) & (g == coal),
                remote(
                    results.at[row, pl.ds(g * 96 if isinstance(g, int) else pl.multiple_of(g * 96, 32), 96)], landed.at[head],
                    o_send.at[row * 4 + g], o_recv.at[head], target,
                ),
            )

        def spread(unit):
            text, latent = unit[:8], unit[8:]
            return jnp.concatenate(([text] * 4 + [latent] * 8) * 4, axis=0)

        def one_row(turn):
            row = lax.rem(y + 1 + turn, YS)
            at_row = pl.ds(pl.multiple_of(row * 16, 16), 16)
            asked = base_q[at_row, :].astype(F32)
            left = spread(asked).astype(BF16)
            full = jnp.concatenate([left, bias_rows[...]], axis=1)
            scores = lax.dot_general(full, text_k[...], nt, preferred_element_type=F32)
            shared = spread(lat_stats[at_row, :])[:, :1]
            maxima = jnp.maximum(jnp.max(scores, axis=1, keepdims=True) * SCALE2, shared)
            weights = jnp.exp2(scores * SCALE2 - maxima).astype(BF16)
            total = jnp.dot(weights, text_v[...], preferred_element_type=F32)
            total = total + jnp.exp2(shared - maxima) * spread(lat_mixed[at_row, :])
            results[row] = (total[:, :HD] / total[:, HD:]).astype(BF16)
            for g in range(4):
                to_self, copy = to_device(row, g)
                if turn < YS - 1:
                    copy.start()
                    continue

                @pl.when(to_self)
                def _():
                    part = results.at[row, pl.ds(g * 96, 96)]
                    pltpu.make_async_copy(part, landed.at[head], o_recv.at[head]).start()

                @pl.when(jnp.logical_not(to_self))
                def _():
                    copy.start()

        for turn in range(YS):
            one_row(turn)

        for copy in second:
            copy.wait_send()
        for copy in crossing:
            copy.wait_send()
        for copy in bias_copies():
            copy.wait_send()

        def drained(step, _):
            to_self, copy = to_device(lax.div(step, 4), lax.rem(step, 4))

            @pl.when(jnp.logical_not(to_self))
            def _():
                copy.wait_send()

            return 0

        lax.fori_loop(0, 16, drained, 0)

    for n in range(len(SHIFTS)):
        for y_to in range(ROWS_Y):
            if SHIFTS[n]:
                remote(*rows_to(n, y_to)).wait_send()
            else:

                @pl.when(jnp.logical_not(in_own & (y == y_to)))
                def _():
                    remote(*rows_to(n, y_to)).wait_send()
                    remote(*queries_to(y_to)).wait_send()

    for head in range(ROWS_Y * XS):
        pltpu.make_async_copy(landed.at[head], landed.at[head], o_recv.at[head]).wait()


def laid_out(landed, out_t, out_l):
    for head in range(ROWS_Y * XS):
        cols = pl.ds(head * HD, HD)
        for pair in range(4):
            unit = widened(landed[head, pair * 8 : pair * 8 + 8, :])
            out_t[2 * pair, :, cols] = unit[:4].astype(BF16)
            out_t[2 * pair + 1, :, cols] = unit[4:].astype(BF16)
        for c in range(8):
            out_l[c, :, cols] = landed[head, 32 + c * 8 : 40 + c * 8, :]


def per_device(lat_q, lat_k, lat_v, txt_q, txt_k, txt_v, span_ids, coal_bits):
    vmem = pl.BlockSpec(memory_space=pltpu.VMEM)
    dma = pltpu.SemaphoreType.DMA
    landed = pl.pallas_call(
        kernel,
        out_shape=pltpu.VMEM((12, 96, HD), BF16),
        in_specs=[pl.BlockSpec(memory_space=pl.ANY)] * 8,
        out_specs=vmem,
        scratch_shapes=[
            pltpu.SMEM((4,), jnp.int32), pltpu.SMEM((8,), jnp.int32),
            pltpu.VMEM((8, 1536), BF16), pltpu.VMEM((8, 1536), BF16), pltpu.VMEM((8, 1536), BF16),
            pltpu.VMEM((4, 1536), BF16), pltpu.VMEM((4, 1536), BF16), pltpu.VMEM((4, 1536), BF16),
            pltpu.VMEM((ROWS_Y, PARTS, 4, HD), BF16),
            pltpu.VMEM((ROWS_Y, 3, 4, HD), BF16),
            pltpu.VMEM((YS, 3, 4, HD), BF16),
            pltpu.VMEM((4, 8, HD), BF16),
            pltpu.VMEM((ZS, 2, YS * PARTS, 4, HD), BF16),
            pltpu.VMEM((512, 2 * HD), BF16),
            pltpu.VMEM((512, 2 * HD), BF16),
            pltpu.VMEM((1024, HD), BF16),
            pltpu.VMEM((1024, 2 * HD), BF16),
            pltpu.VMEM((384, HD), BF16),
            pltpu.VMEM((64, HD), BF16),
            pltpu.VMEM((64, HD), F32),
            pltpu.VMEM((64, 2 * HD), F32),
            pltpu.VMEM((YS, 384, HD), BF16),
            dma((8,)), dma((21,)), dma((28,)), dma((3,)), dma((4,)), dma((3,)), dma((4,)),
            dma((10,)), dma((10,)), dma((16,)), dma((16,)), dma((16,)), dma((12,)),
        ],
        compiler_params=pltpu.CompilerParams(collective_id=0, has_side_effects=True),
        name="coalition_attention",
    )(span_ids, coal_bits, lat_q, lat_k, lat_v, txt_q, txt_k, txt_v)
    return pl.pallas_call(
        laid_out,
        out_shape=(jax.ShapeDtypeStruct((8, 4, 1536), BF16), jax.ShapeDtypeStruct((8, 8, 1536), BF16)),
        in_specs=[vmem],
        out_specs=(vmem, vmem),
        name="laid_out",
    )(landed)


def solution(mesh):
    return jax.shard_map(
        per_device,
        mesh=mesh,
        in_specs=(P("seq", None),) * 6 + (P("seq"), P("coal")),
        out_specs=(P("coal", "seq", None), P("coal", "seq", None)),
        check_vma=False,
    )
```

```python
import functools
import math

import jax
import jax.numpy as jnp
from jax import lax
from jax.experimental import pallas as pl
from jax.experimental.pallas import tpu as pltpu
from jax.sharding import PartitionSpec as P

MESH = pl.DeviceIdType.MESH
BF16, F32 = jnp.bfloat16, jnp.float32

YS, XS, ZS = 4, 4, 16
ROWS_Y = 3
HD = 128
SCALE2 = math.log2(math.e) / math.sqrt(HD)
HIDDEN = -1e30
PARTS = 7
FAR = 5
SHIFTS = (FAR, -FAR, 2, -2, 1, -1, 0)


def place():
    seq, coal = lax.axis_index("seq"), lax.axis_index("coal")
    return lax.div(seq, 32), lax.rem(lax.div(seq, 16), 2), lax.rem(seq, 16), lax.div(coal, 2), lax.rem(coal, 2)


def widened(unit):
    return unit.astype(F32)


def kernel(
    spans_in, bits_in, lq_in, lk_in, lv_in, tq_in, tk_in, tv_in, landed,
    spans, bits, lq, lk, lv, tq, tk, tv,
    own, own_q, queries, biases, gathered, text_k, text_v, lat_k, lat_v, bias_rows, base_q, lat_stats, lat_mixed, results,
    in_sem, s_send, s_recv, q_send, q_recv, b_send, b_recv, z_send, z_recv, c_send, c_recv, o_send, o_recv,
):
    y, x_hi, z, x_lo, core = place()
    x = x_hi * 2 + x_lo
    coal = x_lo * 2 + core
    active = y < ROWS_Y

    z_at = {shift: lax.rem(z + shift + ZS, ZS) for shift in (0, 1, 2, 3, FAR, -1, -2, -3, -FAR)}
    column = y * 32 + x_hi * 16

    def at_z(shift):
        return (column + z_at[shift], coal)

    barrier = pltpu.get_barrier_semaphore()

    def greet(partner):
        pl.semaphore_signal(barrier, inc=1, device_id=partner, device_id_type=MESH)

    in_pair = core == x_hi
    step_x = jnp.where(x_lo == 0, XS - 1, 1)
    x_from = jnp.where(in_pair, x, lax.rem(x + step_x, XS))
    coal_from = lax.rem(x_from, 2) * 2 + jnp.where(in_pair, 0, 1)
    pair_from = lax.div(x_from, 2) * 16
    this = column + z
    others = ((this, x_lo * 2 + 1 - core), (this, (1 - x_lo) * 2 + core), (this, (1 - x_lo) * 2 + 1 - core))

    @pl.when(active)
    def _():
        for shift in SHIFTS:
            for y_from in range(YS):
                greet((pair_from + z_at[-shift] + y_from * 32, coal_from))
        for shift in (1, 2, 3):
            greet(at_z(shift))
            greet(at_z(-shift))
        for other in others:
            greet(other)

    for y_from in range(ROWS_Y):
        for x_of in range(XS):
            greet((z + (y_from * 32 + x_of // 2 * 16), x_hi + x_of % 2 * 2))

    loads = [
        pltpu.make_async_copy(src, dst, in_sem.at[n])
        for n, (src, dst) in enumerate(
            ((spans_in, spans), (bits_in, bits), (tk_in, tk), (tv_in, tv), (lk_in, lk), (lv_in, lv), (tq_in, tq), (lq_in, lq))
        )
    ]
    for load in loads:
        load.start()

    for load in loads:
        load.wait()

    sub = lax.broadcasted_iota(jnp.int32, (8, HD), 0)
    lane = lax.broadcasted_iota(jnp.int32, (8, HD), 1)
    upper = sub < 4
    x_to = jnp.where(core == 0, x, lax.rem(x + step_x, XS))
    pair_to = lax.div(x_to, 2) * 16
    coal_to = lax.rem(x_to, 2) * 2 + x_hi
    span = jnp.zeros((8, HD), jnp.int32)
    for row in range(4):
        span = jnp.where(sub == row, spans[row], span)
    one_hot = jnp.where(lane == span, 1.0, 0.0)[:4]
    for y_to in range(ROWS_Y):
        cols = pl.ds(pl.multiple_of((x_to * ROWS_Y + y_to) * HD, HD), HD)
        keys, values, asked = widened(lk[:, cols]), widened(lv[:, cols]), widened(lq[:, cols])
        own[y_to, 0] = tk[:, cols]
        own[y_to, 1] = tv[:, cols]
        own[y_to, 2] = one_hot.astype(BF16)
        for n in range(2):
            own[y_to, 3 + n] = keys[n * 4 : n * 4 + 4].astype(BF16)
            own[y_to, 5 + n] = values[n * 4 : n * 4 + 4].astype(BF16)
            own_q[y_to, 1 + n] = asked[n * 4 : n * 4 + 4].astype(BF16)
        own_q[y_to, 0] = tq[:, cols]
    kept = jnp.zeros((8, HD), jnp.int32)
    for row in range(8):
        kept = jnp.where(sub == row, bits[row], kept)
    shown = jnp.right_shift(kept, jnp.bitwise_and(lane, 15)) & 1
    biases[coal] = jnp.where((lane < 16) & (shown == 0), HIDDEN, 0.0).astype(BF16)
    text_v[:, HD:] = jnp.ones((512, HD), BF16)
    lat_v[:, HD:] = jnp.ones((1024, HD), BF16)

    in_own = (core == 0) & (x_hi == 0) & active
    pl.semaphore_wait(barrier, len(SHIFTS) * ROWS_Y + jnp.where(active, 6 + 3 + 16, 0))

    def remote(src, dst, send, recv, target):
        return pltpu.make_async_remote_copy(
            src_ref=src, dst_ref=dst, send_sem=send, recv_sem=recv, device_id=target, device_id_type=MESH
        )

    def rows_to(n, y_to):
        target = (pair_to + z_at[SHIFTS[n]] + y_to * 32, coal_to)
        there = gathered.at[-SHIFTS[n] % ZS, x_hi, pl.ds(y * PARTS, PARTS)]
        return (own.at[y_to], there, s_send.at[n * ROWS_Y + y_to], s_recv.at[n * YS + y], target)

    def queries_to(y_to):
        target = (pair_to + z + y_to * 32, coal_to)
        return (own_q.at[y_to], queries.at[y], q_send.at[y_to], q_recv.at[y], target)

    def maybe_own(y_to, copy):
        src, dst, send, recv, target = copy
        to_self = in_own & (y == y_to)

        @pl.when(to_self)
        def _():
            pltpu.make_async_copy(src, dst, recv).start()

        @pl.when(jnp.logical_not(to_self))
        def _():
            remote(src, dst, send, recv, target).start()

    for n in range(len(SHIFTS)):
        for y_to in range(ROWS_Y):
            if SHIFTS[n]:
                remote(*rows_to(n, y_to)).start()
            else:
                maybe_own(y_to, rows_to(n, y_to))
                maybe_own(y_to, queries_to(y_to))

    def bias_copies():
        for n, target in enumerate(others):
            yield remote(biases.at[coal], biases.at[coal], b_send.at[n], b_recv.at[coal], target)

    whole = YS * PARTS

    def ring(n, offset, shift, first=0, count=whole):
        here = gathered.at[offset % ZS, core, pl.ds(first, count)]
        there = gathered.at[(offset - shift) % ZS, core, pl.ds(first, count)]
        return remote(here, there, z_send.at[n], z_recv.at[n], at_z(shift))

    def across(offset):
        block = gathered.at[offset % ZS, core]
        return remote(block, block, c_send.at[offset % ZS], c_recv.at[offset % ZS], others[0])

    half = whole // 2
    forwards = [
        (FAR, -3, half, whole - half), (-FAR, 3, 0, half),
        (FAR, 2), (FAR, -2), (FAR, 1), (FAR, -1), (-FAR, 2), (-FAR, -2), (-FAR, 1), (-FAR, -1),
    ]

    def direct_in(n):
        for y_from in range(YS):
            block = gathered.at[-SHIFTS[n] % ZS, core, pl.ds(y_from * PARTS, PARTS)]
            pltpu.make_async_copy(block, block, s_recv.at[n * YS + y_from]).wait()

    def converted(o):
        for k in range(2):
            part = [[widened(gathered[o, k, n * PARTS + m]) for m in range(PARTS)] for n in range(YS)]

            def rows_of(*which):
                return jnp.concatenate([part[n][m] for n in range(YS) for m in which], axis=0).astype(BF16)

            rows = pl.ds((o * 2 + k) * 16, 16)
            text_k[rows, pl.ds(0, HD)] = rows_of(0)
            text_k[rows, pl.ds(HD, HD)] = rows_of(2)
            text_v[rows, pl.ds(0, HD)] = rows_of(1)
            rows = pl.ds((o * 2 + k) * 32, 32)
            lat_k[rows, :] = rows_of(3, 4)
            lat_v[rows, pl.ds(0, HD)] = rows_of(5, 6)

    nt = (((1,), (1,)), ((), ()))

    @pl.when(active)
    def _():
        for copy in bias_copies():
            copy.start()
        second = [ring(n, *f) for n, f in enumerate(forwards)]
        crossing = [across(o) for o in range(ZS)]
        for n in (0, 1):
            direct_in(n)
            for f, copy in zip(forwards, second):
                if f[0] == -SHIFTS[n]:
                    copy.start()
            crossing[-SHIFTS[n] % ZS].start()
        for n in range(2, len(SHIFTS)):
            direct_in(n)
            crossing[-SHIFTS[n] % ZS].start()

        for n in range(YS):
            pltpu.make_async_copy(queries.at[n], queries.at[n], q_recv.at[n]).wait()
            asked = [widened(queries[n, m]) for m in (0, 0, 1, 2)]
            base_q[pl.ds(n * 16, 16), :] = jnp.concatenate(asked, axis=0).astype(BF16)
        for g in range(4):

            @pl.when(coal != g)
            def _():
                pltpu.make_async_copy(biases.at[g], biases.at[g], b_recv.at[g]).wait()

            unit = widened(biases[g])
            rows = [unit[c : c + 1, :] for c in range(8)]
            parts = [jnp.where(upper, rows[2 * p], rows[2 * p + 1]) for p in range(4)]
            parts += [jnp.broadcast_to(row, (8, HD)) for row in rows]
            bias_rows[pl.ds(g * 96, 96), :] = jnp.concatenate(parts, axis=0).astype(BF16)
        for shift in SHIFTS:
            crossing[-shift % ZS].wait_recv()
            converted(-shift % ZS)
        for n in range(2, len(forwards)):
            second[n].wait_recv()
            crossing[(forwards[n][0] - forwards[n][1]) % ZS].start()
        second[0].wait_recv()
        second[1].wait_recv()
        crossing[8].start()
        for n in list(range(2, len(forwards))) + [0]:
            o = (forwards[n][0] - forwards[n][1]) % ZS
            crossing[o].wait_recv()
            converted(o)

        scores = lax.dot_general(base_q[...], lat_k[...], nt, preferred_element_type=F32) * SCALE2
        maxima = jnp.max(scores, axis=1, keepdims=True)
        weights = jnp.exp2(scores - maxima).astype(BF16)
        lat_stats[...] = jnp.broadcast_to(maxima, (64, HD))
        lat_mixed[...] = jnp.dot(weights, lat_v[...], preferred_element_type=F32)

        head = x * ROWS_Y + y
        near_last = jnp.where(in_pair, x_lo, jnp.where(x_lo == 0, 1, 0))

        def to_device(row, g):
            target = (((row * 2 + core) * ZS + z), g)
            return (
                (row == y) & (core == x_hi) & (g == coal),
                remote(
                    results.at[row, pl.ds(g * 12, 12)], landed.at[head],
                    o_send.at[row * 4 + g], o_recv.at[head], target,
                ),
            )

        def spread(unit):
            text, latent = unit[:8], unit[8:]
            return jnp.concatenate(([text] * 4 + [latent] * 8) * 4, axis=0)

        def one_row(turn):
            row = lax.rem(y + (2, 1, 3, 0)[turn], YS)
            at_row = pl.ds(pl.multiple_of(row * 16, 16), 16)
            asked = base_q[at_row, :].astype(F32)
            left = spread(asked).astype(BF16)
            full = jnp.concatenate([left, bias_rows[...]], axis=1)
            scores = lax.dot_general(full, text_k[...], nt, preferred_element_type=F32)
            shared = spread(lat_stats[at_row, :])[:, :1]
            maxima = jnp.maximum(jnp.max(scores, axis=1, keepdims=True) * SCALE2, shared)
            weights = jnp.exp2(scores * SCALE2 - maxima).astype(BF16)
            total = jnp.dot(weights, text_v[...], preferred_element_type=F32)
            total = total + jnp.exp2(shared - maxima) * spread(lat_mixed[at_row, :])
            results[row] = (total[:, :HD] / total[:, HD:]).reshape(48, 8, HD).astype(BF16)
            for near in range(4):
                g = lax.rem(2 * near_last + near + 2, 4)
                to_self, copy = to_device(row, g)
                if turn < YS - 1:
                    copy.start()
                    continue

                @pl.when(to_self)
                def _():
                    part = results.at[row, pl.ds(g * 12, 12)]
                    pltpu.make_async_copy(part, landed.at[head], o_recv.at[head]).start()

                @pl.when(jnp.logical_not(to_self))
                def _():
                    copy.start()

        for turn in range(YS):
            one_row(turn)

        for copy in second:
            copy.wait_send()
        for copy in crossing:
            copy.wait_send()
        for copy in bias_copies():
            copy.wait_send()

        def drained(step, _):
            to_self, copy = to_device(lax.div(step, 4), lax.rem(step, 4))

            @pl.when(jnp.logical_not(to_self))
            def _():
                copy.wait_send()

            return 0

        lax.fori_loop(0, 16, drained, 0)

    for n in range(len(SHIFTS)):
        for y_to in range(ROWS_Y):
            if SHIFTS[n]:
                remote(*rows_to(n, y_to)).wait_send()
            else:

                @pl.when(jnp.logical_not(in_own & (y == y_to)))
                def _():
                    remote(*rows_to(n, y_to)).wait_send()
                    remote(*queries_to(y_to)).wait_send()

    for head in range(ROWS_Y * XS):
        pltpu.make_async_copy(landed.at[head], landed.at[head], o_recv.at[head]).wait()


def laid_out(landed, out_t, out_l, text, sems):
    copies = []
    for head in range(ROWS_Y * XS):
        cols = pl.ds(head * HD, HD)
        copies.append(pltpu.make_async_copy(landed.at[head, pl.ds(4, 8)], out_l.at[:, :, cols], sems.at[head]))
        copies[-1].start()
    for head in range(ROWS_Y * XS):
        for pair in range(4):
            unit = widened(landed[head, pair])
            text[2 * pair, :, head * HD : (head + 1) * HD] = unit[:4].astype(BF16)
            text[2 * pair + 1, :, head * HD : (head + 1) * HD] = unit[4:].astype(BF16)
    copies.append(pltpu.make_async_copy(text, out_t, sems.at[12]))
    copies[-1].start()
    for copy in copies:
        copy.wait()


def per_device(lat_q, lat_k, lat_v, txt_q, txt_k, txt_v, span_ids, coal_bits):
    vmem = pl.BlockSpec(memory_space=pltpu.VMEM)
    dma = pltpu.SemaphoreType.DMA
    landed = pl.pallas_call(
        kernel,
        out_shape=pltpu.VMEM((12, 12, 8, HD), BF16),
        in_specs=[pl.BlockSpec(memory_space=pl.ANY)] * 8,
        out_specs=vmem,
        scratch_shapes=[
            pltpu.SMEM((4,), jnp.int32), pltpu.SMEM((8,), jnp.int32),
            pltpu.VMEM((8, 1536), BF16), pltpu.VMEM((8, 1536), BF16), pltpu.VMEM((8, 1536), BF16),
            pltpu.VMEM((4, 1536), BF16), pltpu.VMEM((4, 1536), BF16), pltpu.VMEM((4, 1536), BF16),
            pltpu.VMEM((ROWS_Y, PARTS, 4, HD), BF16),
            pltpu.VMEM((ROWS_Y, 3, 4, HD), BF16),
            pltpu.VMEM((YS, 3, 4, HD), BF16),
            pltpu.VMEM((4, 8, HD), BF16),
            pltpu.VMEM((ZS, 2, YS * PARTS, 4, HD), BF16),
            pltpu.VMEM((512, 2 * HD), BF16),
            pltpu.VMEM((512, 2 * HD), BF16),
            pltpu.VMEM((1024, HD), BF16),
            pltpu.VMEM((1024, 2 * HD), BF16),
            pltpu.VMEM((384, HD), BF16),
            pltpu.VMEM((64, HD), BF16),
            pltpu.VMEM((64, HD), F32),
            pltpu.VMEM((64, 2 * HD), F32),
            pltpu.VMEM((YS, 48, 8, HD), BF16),
            dma((8,)), dma((21,)), dma((28,)), dma((3,)), dma((4,)), dma((3,)), dma((4,)),
            dma((10,)), dma((10,)), dma((16,)), dma((16,)), dma((16,)), dma((12,)),
        ],
        compiler_params=pltpu.CompilerParams(collective_id=0, has_side_effects=True),
        name="coalition_attention",
    )(span_ids, coal_bits, lat_q, lat_k, lat_v, txt_q, txt_k, txt_v)
    return pl.pallas_call(
        laid_out,
        out_shape=(jax.ShapeDtypeStruct((8, 4, 1536), BF16), jax.ShapeDtypeStruct((8, 8, 1536), BF16)),
        in_specs=[vmem],
        out_specs=(pl.BlockSpec(memory_space=pl.ANY),) * 2,
        scratch_shapes=[pltpu.VMEM((8, 4, 1536), BF16), dma((13,))],
        name="laid_out",
    )(pltpu.with_memory_space_constraint(landed, pltpu.VMEM))


def solution(mesh):
    return jax.shard_map(
        per_device,
        mesh=mesh,
        in_specs=(P("seq", None),) * 6 + (P("seq"), P("coal")),
        out_specs=(P("coal", "seq", None), P("coal", "seq", None)),
        check_vma=False,
    )
```

```python
import functools
import math

import jax
import jax.numpy as jnp
from jax import lax
from jax.experimental import pallas as pl
from jax.experimental.pallas import tpu as pltpu
from jax.sharding import PartitionSpec as P

MESH = pl.DeviceIdType.MESH
BF16, F32 = jnp.bfloat16, jnp.float32

YS, XS, ZS = 4, 4, 16
ROWS_Y = 3
HD = 128
SCALE2 = math.log2(math.e) / math.sqrt(HD)
HIDDEN = -1e30
PARTS = 7
FAR = 5
SHIFTS = (FAR, -FAR, 3, -3, 2, -2, 1, -1, 0)


def place():
    seq, coal = lax.axis_index("seq"), lax.axis_index("coal")
    return lax.div(seq, 32), lax.rem(lax.div(seq, 16), 2), lax.rem(seq, 16), lax.div(coal, 2), lax.rem(coal, 2)


def widened(unit):
    return unit.astype(F32)


def kernel(
    spans_in, bits_in, lq_in, lk_in, lv_in, tq_in, tk_in, tv_in, landed,
    spans, bits, lq, lk, lv, tq, tk, tv,
    own, own_q, queries, biases, gathered, text_k, text_v, lat_k, lat_v, bias_rows, base_q, lat_stats, lat_mixed, results,
    in_sem, s_send, s_recv, q_send, q_recv, b_send, b_recv, z_send, z_recv, c_send, c_recv, o_send, o_recv,
):
    y, x_hi, z, x_lo, core = place()
    x = x_hi * 2 + x_lo
    coal = x_lo * 2 + core
    active = y < ROWS_Y

    z_at = {shift: lax.rem(z + shift + ZS, ZS) for shift in (0, 1, 2, 3, FAR, -1, -2, -3, -FAR)}
    column = y * 32 + x_hi * 16

    def at_z(shift):
        return (column + z_at[shift], coal)

    barrier = pltpu.get_barrier_semaphore()

    def greet(partner):
        pl.semaphore_signal(barrier, inc=1, device_id=partner, device_id_type=MESH)

    in_pair = core == x_hi
    step_x = jnp.where(x_lo == 0, XS - 1, 1)
    x_from = jnp.where(in_pair, x, lax.rem(x + step_x, XS))
    coal_from = lax.rem(x_from, 2) * 2 + jnp.where(in_pair, 0, 1)
    pair_from = lax.div(x_from, 2) * 16
    this = column + z
    others = ((this, x_lo * 2 + 1 - core), (this, (1 - x_lo) * 2 + core), (this, (1 - x_lo) * 2 + 1 - core))

    @pl.when(active)
    def _():
        for shift in SHIFTS:
            for y_from in range(YS):
                greet((pair_from + z_at[-shift] + y_from * 32, coal_from))
        for shift in (1, 2, 3):
            greet(at_z(shift))
            greet(at_z(-shift))
        for other in others:
            greet(other)

    for y_from in range(ROWS_Y):
        for x_of in range(XS):
            greet((z + (y_from * 32 + x_of // 2 * 16), x_hi + x_of % 2 * 2))

    loads = [
        pltpu.make_async_copy(src, dst, in_sem.at[n])
        for n, (src, dst) in enumerate(
            ((spans_in, spans), (bits_in, bits), (tk_in, tk), (tv_in, tv), (lk_in, lk), (lv_in, lv), (tq_in, tq), (lq_in, lq))
        )
    ]
    for load in loads:
        load.start()

    for load in loads:
        load.wait()

    sub = lax.broadcasted_iota(jnp.int32, (8, HD), 0)
    lane = lax.broadcasted_iota(jnp.int32, (8, HD), 1)
    upper = sub < 4
    x_to = jnp.where(core == 0, x, lax.rem(x + step_x, XS))
    pair_to = lax.div(x_to, 2) * 16
    coal_to = lax.rem(x_to, 2) * 2 + x_hi
    span = jnp.zeros((8, HD), jnp.int32)
    for row in range(4):
        span = jnp.where(sub == row, spans[row], span)
    one_hot = jnp.where(lane == span, 1.0, 0.0)[:4]
    for y_to in range(ROWS_Y):
        cols = pl.ds(pl.multiple_of((x_to * ROWS_Y + y_to) * HD, HD), HD)
        keys, values, asked = widened(lk[:, cols]), widened(lv[:, cols]), widened(lq[:, cols])
        own[y_to, 0] = tk[:, cols]
        own[y_to, 1] = tv[:, cols]
        own[y_to, 2] = one_hot.astype(BF16)
        for n in range(2):
            own[y_to, 3 + n] = keys[n * 4 : n * 4 + 4].astype(BF16)
            own[y_to, 5 + n] = values[n * 4 : n * 4 + 4].astype(BF16)
            own_q[y_to, 1 + n] = asked[n * 4 : n * 4 + 4].astype(BF16)
        own_q[y_to, 0] = tq[:, cols]
    kept = jnp.zeros((8, HD), jnp.int32)
    for row in range(8):
        kept = jnp.where(sub == row, bits[row], kept)
    shown = jnp.right_shift(kept, jnp.bitwise_and(lane, 15)) & 1
    biases[coal] = jnp.where((lane < 16) & (shown == 0), HIDDEN, 0.0).astype(BF16)
    text_v[:, HD:] = jnp.ones((512, HD), BF16)
    lat_v[:, HD:] = jnp.ones((1024, HD), BF16)

    in_own = (core == 0) & (x_hi == 0) & active
    pl.semaphore_wait(barrier, len(SHIFTS) * ROWS_Y + jnp.where(active, 6 + 3 + 16, 0))

    def remote(src, dst, send, recv, target):
        return pltpu.make_async_remote_copy(
            src_ref=src, dst_ref=dst, send_sem=send, recv_sem=recv, device_id=target, device_id_type=MESH
        )

    def rows_to(n, y_to):
        target = (pair_to + z_at[SHIFTS[n]] + y_to * 32, coal_to)
        there = gathered.at[-SHIFTS[n] % ZS, x_hi, pl.ds(y * PARTS, PARTS)]
        return (own.at[y_to], there, s_send.at[n * ROWS_Y + y_to], s_recv.at[n * YS + y], target)

    def queries_to(y_to):
        target = (pair_to + z + y_to * 32, coal_to)
        return (own_q.at[y_to], queries.at[y], q_send.at[y_to], q_recv.at[y], target)

    def maybe_own(y_to, copy):
        src, dst, send, recv, target = copy
        to_self = in_own & (y == y_to)

        @pl.when(to_self)
        def _():
            pltpu.make_async_copy(src, dst, recv).start()

        @pl.when(jnp.logical_not(to_self))
        def _():
            remote(src, dst, send, recv, target).start()

    for n in range(len(SHIFTS)):
        for y_to in range(ROWS_Y):
            if SHIFTS[n]:
                remote(*rows_to(n, y_to)).start()
            else:
                maybe_own(y_to, rows_to(n, y_to))
                maybe_own(y_to, queries_to(y_to))

    def bias_copies():
        for n, target in enumerate(others):
            yield remote(biases.at[coal], biases.at[coal], b_send.at[n], b_recv.at[coal], target)

    whole = YS * PARTS

    def ring(n, offset, shift, first=0, count=whole):
        here = gathered.at[offset % ZS, core, pl.ds(first, count)]
        there = gathered.at[(offset - shift) % ZS, core, pl.ds(first, count)]
        return remote(here, there, z_send.at[n], z_recv.at[n], at_z(shift))

    def across(offset):
        block = gathered.at[offset % ZS, core]
        return remote(block, block, c_send.at[offset % ZS], c_recv.at[offset % ZS], others[0])

    half = whole // 2
    forwards = [
        (FAR, -3, half, whole - half), (-FAR, 3, 0, half),
        (FAR, -2), (-FAR, 2), (FAR, 1), (FAR, -1), (-FAR, 1), (-FAR, -1),
    ]

    def direct_in(n):
        for y_from in range(YS):
            block = gathered.at[-SHIFTS[n] % ZS, core, pl.ds(y_from * PARTS, PARTS)]
            pltpu.make_async_copy(block, block, s_recv.at[n * YS + y_from]).wait()

    def converted(o):
        for k in range(2):
            part = [[widened(gathered[o, k, n * PARTS + m]) for m in range(PARTS)] for n in range(YS)]

            def rows_of(*which):
                return jnp.concatenate([part[n][m] for n in range(YS) for m in which], axis=0).astype(BF16)

            rows = pl.ds((o * 2 + k) * 16, 16)
            text_k[rows, pl.ds(0, HD)] = rows_of(0)
            text_k[rows, pl.ds(HD, HD)] = rows_of(2)
            text_v[rows, pl.ds(0, HD)] = rows_of(1)
            rows = pl.ds((o * 2 + k) * 32, 32)
            lat_k[rows, :] = rows_of(3, 4)
            lat_v[rows, pl.ds(0, HD)] = rows_of(5, 6)

    nt = (((1,), (1,)), ((), ()))

    @pl.when(active)
    def _():
        for copy in bias_copies():
            copy.start()
        second = [ring(n, *f) for n, f in enumerate(forwards)]
        crossing = [across(o) for o in range(ZS)]
        for n in (0, 1):
            direct_in(n)
            for f, copy in zip(forwards, second):
                if f[0] == -SHIFTS[n]:
                    copy.start()
            crossing[-SHIFTS[n] % ZS].start()
        for n in range(2, len(SHIFTS)):
            direct_in(n)
            crossing[-SHIFTS[n] % ZS].start()

        for n in range(YS):
            pltpu.make_async_copy(queries.at[n], queries.at[n], q_recv.at[n]).wait()
            asked = [widened(queries[n, m]) for m in (0, 0, 1, 2)]
            base_q[pl.ds(n * 16, 16), :] = jnp.concatenate(asked, axis=0).astype(BF16)
        for g in range(4):

            @pl.when(coal != g)
            def _():
                pltpu.make_async_copy(biases.at[g], biases.at[g], b_recv.at[g]).wait()

            unit = widened(biases[g])
            rows = [unit[c : c + 1, :] for c in range(8)]
            parts = [jnp.where(upper, rows[2 * p], rows[2 * p + 1]) for p in range(4)]
            parts += [jnp.broadcast_to(row, (8, HD)) for row in rows]
            bias_rows[pl.ds(g * 96, 96), :] = jnp.concatenate(parts, axis=0).astype(BF16)
        for shift in SHIFTS:
            crossing[-shift % ZS].wait_recv()
            converted(-shift % ZS)
        for n in range(2, len(forwards)):
            second[n].wait_recv()
            crossing[(forwards[n][0] - forwards[n][1]) % ZS].start()
        second[0].wait_recv()
        second[1].wait_recv()
        crossing[8].start()
        for n in list(range(2, len(forwards))) + [0]:
            o = (forwards[n][0] - forwards[n][1]) % ZS
            crossing[o].wait_recv()
            converted(o)

        scores = lax.dot_general(base_q[...], lat_k[...], nt, preferred_element_type=F32) * SCALE2
        maxima = jnp.max(scores, axis=1, keepdims=True)
        weights = jnp.exp2(scores - maxima).astype(BF16)
        lat_stats[...] = jnp.broadcast_to(maxima, (64, HD))
        lat_mixed[...] = jnp.dot(weights, lat_v[...], preferred_element_type=F32)

        head = x * ROWS_Y + y
        near_last = jnp.where(in_pair, x_lo, jnp.where(x_lo == 0, 1, 0))

        def to_device(row, g):
            target = (((row * 2 + core) * ZS + z), g)
            return (
                (row == y) & (core == x_hi) & (g == coal),
                remote(
                    results.at[row, pl.ds(g * 12, 12)], landed.at[head],
                    o_send.at[row * 4 + g], o_recv.at[head], target,
                ),
            )

        def spread(unit):
            text, latent = unit[:8], unit[8:]
            return jnp.concatenate(([text] * 4 + [latent] * 8) * 4, axis=0)

        def one_row(turn):
            row = lax.rem(y + (2, 1, 3, 0)[turn], YS)
            at_row = pl.ds(pl.multiple_of(row * 16, 16), 16)
            asked = base_q[at_row, :].astype(F32)
            left = spread(asked).astype(BF16)
            full = jnp.concatenate([left, bias_rows[...]], axis=1)
            scores = lax.dot_general(full, text_k[...], nt, preferred_element_type=F32)
            shared = spread(lat_stats[at_row, :])[:, :1]
            maxima = jnp.maximum(jnp.max(scores, axis=1, keepdims=True) * SCALE2, shared)
            weights = jnp.exp2(scores * SCALE2 - maxima).astype(BF16)
            total = jnp.dot(weights, text_v[...], preferred_element_type=F32)
            total = total + jnp.exp2(shared - maxima) * spread(lat_mixed[at_row, :])
            results[row] = (total[:, :HD] / total[:, HD:]).reshape(48, 8, HD).astype(BF16)
            for near in range(4):
                g = lax.rem(2 * near_last + near + 2, 4)
                to_self, copy = to_device(row, g)
                if turn < YS - 1:
                    copy.start()
                    continue

                @pl.when(to_self)
                def _():
                    part = results.at[row, pl.ds(g * 12, 12)]
                    pltpu.make_async_copy(part, landed.at[head], o_recv.at[head]).start()

                @pl.when(jnp.logical_not(to_self))
                def _():
                    copy.start()

        for turn in range(YS):
            one_row(turn)

        for copy in second:
            copy.wait_send()
        for copy in crossing:
            copy.wait_send()
        for copy in bias_copies():
            copy.wait_send()

        def drained(step, _):
            to_self, copy = to_device(lax.div(step, 4), lax.rem(step, 4))

            @pl.when(jnp.logical_not(to_self))
            def _():
                copy.wait_send()

            return 0

        lax.fori_loop(0, 16, drained, 0)

    for n in range(len(SHIFTS)):
        for y_to in range(ROWS_Y):
            if SHIFTS[n]:
                remote(*rows_to(n, y_to)).wait_send()
            else:

                @pl.when(jnp.logical_not(in_own & (y == y_to)))
                def _():
                    remote(*rows_to(n, y_to)).wait_send()
                    remote(*queries_to(y_to)).wait_send()

    for head in range(ROWS_Y * XS):
        pltpu.make_async_copy(landed.at[head], landed.at[head], o_recv.at[head]).wait()


def laid_out(landed, out_t, out_l, text, sems):
    copies = []
    for head in range(ROWS_Y * XS):
        cols = pl.ds(head * HD, HD)
        copies.append(pltpu.make_async_copy(landed.at[head, pl.ds(4, 8)], out_l.at[:, :, cols], sems.at[head]))
        copies[-1].start()
    for head in range(ROWS_Y * XS):
        for pair in range(4):
            unit = widened(landed[head, pair])
            text[2 * pair, :, head * HD : (head + 1) * HD] = unit[:4].astype(BF16)
            text[2 * pair + 1, :, head * HD : (head + 1) * HD] = unit[4:].astype(BF16)
    copies.append(pltpu.make_async_copy(text, out_t, sems.at[12]))
    copies[-1].start()
    for copy in copies:
        copy.wait()


def per_device(lat_q, lat_k, lat_v, txt_q, txt_k, txt_v, span_ids, coal_bits):
    vmem = pl.BlockSpec(memory_space=pltpu.VMEM)
    dma = pltpu.SemaphoreType.DMA
    landed = pl.pallas_call(
        kernel,
        out_shape=pltpu.VMEM((12, 12, 8, HD), BF16),
        in_specs=[pl.BlockSpec(memory_space=pl.ANY)] * 8,
        out_specs=vmem,
        scratch_shapes=[
            pltpu.SMEM((4,), jnp.int32), pltpu.SMEM((8,), jnp.int32),
            pltpu.VMEM((8, 1536), BF16), pltpu.VMEM((8, 1536), BF16), pltpu.VMEM((8, 1536), BF16),
            pltpu.VMEM((4, 1536), BF16), pltpu.VMEM((4, 1536), BF16), pltpu.VMEM((4, 1536), BF16),
            pltpu.VMEM((ROWS_Y, PARTS, 4, HD), BF16),
            pltpu.VMEM((ROWS_Y, 3, 4, HD), BF16),
            pltpu.VMEM((YS, 3, 4, HD), BF16),
            pltpu.VMEM((4, 8, HD), BF16),
            pltpu.VMEM((ZS, 2, YS * PARTS, 4, HD), BF16),
            pltpu.VMEM((512, 2 * HD), BF16),
            pltpu.VMEM((512, 2 * HD), BF16),
            pltpu.VMEM((1024, HD), BF16),
            pltpu.VMEM((1024, 2 * HD), BF16),
            pltpu.VMEM((384, HD), BF16),
            pltpu.VMEM((64, HD), BF16),
            pltpu.VMEM((64, HD), F32),
            pltpu.VMEM((64, 2 * HD), F32),
            pltpu.VMEM((YS, 48, 8, HD), BF16),
            dma((8,)), dma((27,)), dma((36,)), dma((3,)), dma((4,)), dma((3,)), dma((4,)),
            dma((8,)), dma((8,)), dma((16,)), dma((16,)), dma((16,)), dma((12,)),
        ],
        compiler_params=pltpu.CompilerParams(collective_id=0, has_side_effects=True),
        name="coalition_attention",
    )(span_ids, coal_bits, lat_q, lat_k, lat_v, txt_q, txt_k, txt_v)
    return pl.pallas_call(
        laid_out,
        out_shape=(jax.ShapeDtypeStruct((8, 4, 1536), BF16), jax.ShapeDtypeStruct((8, 8, 1536), BF16)),
        in_specs=[vmem],
        out_specs=(pl.BlockSpec(memory_space=pl.ANY),) * 2,
        scratch_shapes=[pltpu.VMEM((8, 4, 1536), BF16), dma((13,))],
        name="laid_out",
    )(pltpu.with_memory_space_constraint(landed, pltpu.VMEM))


def solution(mesh):
    return jax.shard_map(
        per_device,
        mesh=mesh,
        in_specs=(P("seq", None),) * 6 + (P("seq"), P("coal")),
        out_specs=(P("coal", "seq", None), P("coal", "seq", None)),
        check_vma=False,
    )
```

```python
import functools
import math

import jax
import jax.numpy as jnp
from jax import lax
from jax.experimental import pallas as pl
from jax.experimental.pallas import tpu as pltpu
from jax.sharding import PartitionSpec as P

MESH = pl.DeviceIdType.MESH
BF16, F32 = jnp.bfloat16, jnp.float32

YS, XS, ZS = 4, 4, 16
ROWS_Y = 3
HD = 128
SCALE2 = math.log2(math.e) / math.sqrt(HD)
HIDDEN = -1e30
PARTS = 7
FAR = 5
SHIFTS = (0, FAR, -FAR)


def place():
    seq, coal = lax.axis_index("seq"), lax.axis_index("coal")
    return lax.div(seq, 32), lax.rem(lax.div(seq, 16), 2), lax.rem(seq, 16), lax.div(coal, 2), lax.rem(coal, 2)


def widened(unit):
    return unit.astype(F32)


def kernel(
    spans_in, bits_in, lq_in, lk_in, lv_in, tq_in, tk_in, tv_in, landed,
    spans, bits, lq, lk, lv, tq, tk, tv,
    own, own_q, queries, biases, gathered, text_k, text_v, lat_k, lat_v, bias_rows, base_q, lat_stats, lat_mixed, results,
    in_sem, s_send, s_recv, q_send, q_recv, b_send, b_recv, z_send, z_recv, c_send, c_recv, o_send, o_recv,
):
    y, x_hi, z, x_lo, core = place()
    x = x_hi * 2 + x_lo
    coal = x_lo * 2 + core
    active = y < ROWS_Y

    z_at = {shift: lax.rem(z + shift + ZS, ZS) for shift in (0, 1, 2, 3, FAR, -1, -2, -3, -FAR)}
    column = y * 32 + x_hi * 16

    def at_z(shift):
        return (column + z_at[shift], coal)

    barrier = pltpu.get_barrier_semaphore()

    def greet(partner):
        pl.semaphore_signal(barrier, inc=1, device_id=partner, device_id_type=MESH)

    in_pair = core == x_hi
    step_x = jnp.where(x_lo == 0, XS - 1, 1)
    x_from = jnp.where(in_pair, x, lax.rem(x + step_x, XS))
    coal_from = lax.rem(x_from, 2) * 2 + jnp.where(in_pair, 0, 1)
    pair_from = lax.div(x_from, 2) * 16
    this = column + z
    others = ((this, x_lo * 2 + 1 - core), (this, (1 - x_lo) * 2 + core), (this, (1 - x_lo) * 2 + 1 - core))

    @pl.when(active)
    def _():
        for shift in SHIFTS:
            for y_from in range(YS):
                greet((pair_from + z_at[-shift] + y_from * 32, coal_from))
        for shift in (1, 2, 3):
            greet(at_z(shift))
            greet(at_z(-shift))
        for other in others:
            greet(other)

    for y_from in range(ROWS_Y):
        for x_of in range(XS):
            greet((z + (y_from * 32 + x_of // 2 * 16), x_hi + x_of % 2 * 2))

    loads = [
        pltpu.make_async_copy(src, dst, in_sem.at[n])
        for n, (src, dst) in enumerate(
            ((spans_in, spans), (bits_in, bits), (tk_in, tk), (tv_in, tv), (lk_in, lk), (lv_in, lv), (tq_in, tq), (lq_in, lq))
        )
    ]
    for load in loads:
        load.start()

    for load in loads:
        load.wait()

    sub = lax.broadcasted_iota(jnp.int32, (8, HD), 0)
    lane = lax.broadcasted_iota(jnp.int32, (8, HD), 1)
    upper = sub < 4
    x_to = jnp.where(core == 0, x, lax.rem(x + step_x, XS))
    pair_to = lax.div(x_to, 2) * 16
    coal_to = lax.rem(x_to, 2) * 2 + x_hi
    span = jnp.zeros((8, HD), jnp.int32)
    for row in range(4):
        span = jnp.where(sub == row, spans[row], span)
    one_hot = jnp.where(lane == span, 1.0, 0.0)[:4]
    for y_to in range(ROWS_Y):
        cols = pl.ds(pl.multiple_of((x_to * ROWS_Y + y_to) * HD, HD), HD)
        keys, values, asked = widened(lk[:, cols]), widened(lv[:, cols]), widened(lq[:, cols])
        own[y_to, 0] = tk[:, cols]
        own[y_to, 1] = tv[:, cols]
        own[y_to, 2] = one_hot.astype(BF16)
        for n in range(2):
            own[y_to, 3 + n] = keys[n * 4 : n * 4 + 4].astype(BF16)
            own[y_to, 5 + n] = values[n * 4 : n * 4 + 4].astype(BF16)
            own_q[y_to, 1 + n] = asked[n * 4 : n * 4 + 4].astype(BF16)
        own_q[y_to, 0] = tq[:, cols]
    kept = jnp.zeros((8, HD), jnp.int32)
    for row in range(8):
        kept = jnp.where(sub == row, bits[row], kept)
    shown = jnp.right_shift(kept, jnp.bitwise_and(lane, 15)) & 1
    biases[coal] = jnp.where((lane < 16) & (shown == 0), HIDDEN, 0.0).astype(BF16)
    text_v[:, HD:] = jnp.ones((512, HD), BF16)
    lat_v[:, HD:] = jnp.ones((1024, HD), BF16)

    in_own = (core == 0) & (x_hi == 0) & active
    pl.semaphore_wait(barrier, len(SHIFTS) * ROWS_Y + jnp.where(active, 6 + 3 + 16, 0))

    def remote(src, dst, send, recv, target):
        return pltpu.make_async_remote_copy(
            src_ref=src, dst_ref=dst, send_sem=send, recv_sem=recv, device_id=target, device_id_type=MESH
        )

    def rows_to(n, y_to):
        target = (pair_to + z_at[SHIFTS[n]] + y_to * 32, coal_to)
        there = gathered.at[-SHIFTS[n] % ZS, x_hi, pl.ds(y * PARTS, PARTS)]
        return (own.at[y_to], there, s_send.at[n * ROWS_Y + y_to], s_recv.at[n * YS + y], target)

    def queries_to(y_to):
        target = (pair_to + z + y_to * 32, coal_to)
        return (own_q.at[y_to], queries.at[y], q_send.at[y_to], q_recv.at[y], target)

    def maybe_own(y_to, copy):
        src, dst, send, recv, target = copy
        to_self = in_own & (y == y_to)

        @pl.when(to_self)
        def _():
            pltpu.make_async_copy(src, dst, recv).start()

        @pl.when(jnp.logical_not(to_self))
        def _():
            remote(src, dst, send, recv, target).start()

    for n in (1, 2, 0):
        for y_to in range(ROWS_Y):
            if SHIFTS[n]:
                remote(*rows_to(n, y_to)).start()
            else:
                maybe_own(y_to, rows_to(n, y_to))
                maybe_own(y_to, queries_to(y_to))

    def bias_copies():
        for n, target in enumerate(others):
            yield remote(biases.at[coal], biases.at[coal], b_send.at[n], b_recv.at[coal], target)

    whole = YS * PARTS

    def ring(n, offset, shift, first=0, count=whole):
        here = gathered.at[offset % ZS, core, pl.ds(first, count)]
        there = gathered.at[(offset - shift) % ZS, core, pl.ds(first, count)]
        return remote(here, there, z_send.at[n], z_recv.at[n], at_z(shift))

    def across(offset):
        block = gathered.at[offset % ZS, core]
        return remote(block, block, c_send.at[offset % ZS], c_recv.at[offset % ZS], others[0])

    half = whole // 2
    forwards = [
        (0, 3), (0, -3), (0, 2), (0, -2), (0, 1), (0, -1),
        (FAR, -3, half, whole - half), (-FAR, 3, 0, half),
        (FAR, -2), (-FAR, 2), (FAR, 1), (FAR, -1), (-FAR, 1), (-FAR, -1),
    ]

    def direct_in(n):
        for y_from in range(YS):
            block = gathered.at[-SHIFTS[n] % ZS, core, pl.ds(y_from * PARTS, PARTS)]
            pltpu.make_async_copy(block, block, s_recv.at[n * YS + y_from]).wait()

    def converted(o):
        for k in range(2):
            part = [[widened(gathered[o, k, n * PARTS + m]) for m in range(PARTS)] for n in range(YS)]

            def rows_of(*which):
                return jnp.concatenate([part[n][m] for n in range(YS) for m in which], axis=0).astype(BF16)

            rows = pl.ds((o * 2 + k) * 16, 16)
            text_k[rows, pl.ds(0, HD)] = rows_of(0)
            text_k[rows, pl.ds(HD, HD)] = rows_of(2)
            text_v[rows, pl.ds(0, HD)] = rows_of(1)
            rows = pl.ds((o * 2 + k) * 32, 32)
            lat_k[rows, :] = rows_of(3, 4)
            lat_v[rows, pl.ds(0, HD)] = rows_of(5, 6)

    nt = (((1,), (1,)), ((), ()))

    @pl.when(active)
    def _():
        for copy in bias_copies():
            copy.start()
        second = [ring(n, *f) for n, f in enumerate(forwards)]
        crossing = [across(o) for o in range(ZS)]
        def arrived(n):
            second[n].wait_recv()
            offset = (forwards[n][0] - forwards[n][1]) % ZS
            if offset != 8:
                crossing[offset].start()
            return offset

        for n in range(len(SHIFTS)):
            direct_in(n)
            for f, copy in zip(forwards, second):
                if f[0] == -SHIFTS[n]:
                    copy.start()
            crossing[-SHIFTS[n] % ZS].start()
        early = [0, FAR, ZS - FAR] + [arrived(n) for n in (4, 5, 2, 3, 0, 1)]

        for n in range(YS):
            pltpu.make_async_copy(queries.at[n], queries.at[n], q_recv.at[n]).wait()
            asked = [widened(queries[n, m]) for m in (0, 0, 1, 2)]
            base_q[pl.ds(n * 16, 16), :] = jnp.concatenate(asked, axis=0).astype(BF16)
        for g in range(4):

            @pl.when(coal != g)
            def _():
                pltpu.make_async_copy(biases.at[g], biases.at[g], b_recv.at[g]).wait()

            unit = widened(biases[g])
            rows = [unit[c : c + 1, :] for c in range(8)]
            parts = [jnp.where(upper, rows[2 * p], rows[2 * p + 1]) for p in range(4)]
            parts += [jnp.broadcast_to(row, (8, HD)) for row in rows]
            bias_rows[pl.ds(g * 96, 96), :] = jnp.concatenate(parts, axis=0).astype(BF16)
        for offset in early:
            crossing[offset].wait_recv()
            converted(offset)
        late = [arrived(n) for n in range(8, 14)] + [8]
        second[6].wait_recv()
        second[7].wait_recv()
        crossing[8].start()
        for offset in late:
            crossing[offset].wait_recv()
            converted(offset)

        scores = lax.dot_general(base_q[...], lat_k[...], nt, preferred_element_type=F32) * SCALE2
        maxima = jnp.max(scores, axis=1, keepdims=True)
        weights = jnp.exp2(scores - maxima).astype(BF16)
        lat_stats[...] = jnp.broadcast_to(maxima, (64, HD))
        lat_mixed[...] = jnp.dot(weights, lat_v[...], preferred_element_type=F32)

        head = x * ROWS_Y + y
        near_last = jnp.where(in_pair, x_lo, jnp.where(x_lo == 0, 1, 0))

        def to_device(row, g):
            target = (((row * 2 + core) * ZS + z), g)
            return (
                (row == y) & (core == x_hi) & (g == coal),
                remote(
                    results.at[row, pl.ds(g * 12, 12)], landed.at[head],
                    o_send.at[row * 4 + g], o_recv.at[head], target,
                ),
            )

        def spread(unit):
            text, latent = unit[:8], unit[8:]
            return jnp.concatenate(([text] * 4 + [latent] * 8) * 4, axis=0)

        def one_row(turn):
            row = lax.rem(y + (2, 1, 3, 0)[turn], YS)
            at_row = pl.ds(pl.multiple_of(row * 16, 16), 16)
            asked = base_q[at_row, :].astype(F32)
            left = spread(asked).astype(BF16)
            full = jnp.concatenate([left, bias_rows[...]], axis=1)
            scores = lax.dot_general(full, text_k[...], nt, preferred_element_type=F32)
            shared = spread(lat_stats[at_row, :])[:, :1]
            maxima = jnp.maximum(jnp.max(scores, axis=1, keepdims=True) * SCALE2, shared)
            weights = jnp.exp2(scores * SCALE2 - maxima).astype(BF16)
            total = jnp.dot(weights, text_v[...], preferred_element_type=F32)
            total = total + jnp.exp2(shared - maxima) * spread(lat_mixed[at_row, :])
            results[row] = (total[:, :HD] / total[:, HD:]).reshape(48, 8, HD).astype(BF16)
            for near in range(4):
                g = lax.rem(2 * near_last + near + 2, 4)
                to_self, copy = to_device(row, g)
                if turn < YS - 1:
                    copy.start()
                    continue

                @pl.when(to_self)
                def _():
                    part = results.at[row, pl.ds(g * 12, 12)]
                    pltpu.make_async_copy(part, landed.at[head], o_recv.at[head]).start()

                @pl.when(jnp.logical_not(to_self))
                def _():
                    copy.start()

        for turn in range(YS):
            one_row(turn)

        for copy in second:
            copy.wait_send()
        for copy in crossing:
            copy.wait_send()
        for copy in bias_copies():
            copy.wait_send()

        def drained(step, _):
            to_self, copy = to_device(lax.div(step, 4), lax.rem(step, 4))

            @pl.when(jnp.logical_not(to_self))
            def _():
                copy.wait_send()

            return 0

        lax.fori_loop(0, 16, drained, 0)

    for n in range(len(SHIFTS)):
        for y_to in range(ROWS_Y):
            if SHIFTS[n]:
                remote(*rows_to(n, y_to)).wait_send()
            else:

                @pl.when(jnp.logical_not(in_own & (y == y_to)))
                def _():
                    remote(*rows_to(n, y_to)).wait_send()
                    remote(*queries_to(y_to)).wait_send()

    for head in range(ROWS_Y * XS):
        pltpu.make_async_copy(landed.at[head], landed.at[head], o_recv.at[head]).wait()


def laid_out(landed, out_t, out_l, text, sems):
    copies = []
    for head in range(ROWS_Y * XS):
        cols = pl.ds(head * HD, HD)
        copies.append(pltpu.make_async_copy(landed.at[head, pl.ds(4, 8)], out_l.at[:, :, cols], sems.at[head]))
        copies[-1].start()
    for head in range(ROWS_Y * XS):
        for pair in range(4):
            unit = widened(landed[head, pair])
            text[2 * pair, :, head * HD : (head + 1) * HD] = unit[:4].astype(BF16)
            text[2 * pair + 1, :, head * HD : (head + 1) * HD] = unit[4:].astype(BF16)
    copies.append(pltpu.make_async_copy(text, out_t, sems.at[12]))
    copies[-1].start()
    for copy in copies:
        copy.wait()


def per_device(lat_q, lat_k, lat_v, txt_q, txt_k, txt_v, span_ids, coal_bits):
    vmem = pl.BlockSpec(memory_space=pltpu.VMEM)
    dma = pltpu.SemaphoreType.DMA
    landed = pl.pallas_call(
        kernel,
        out_shape=pltpu.VMEM((12, 12, 8, HD), BF16),
        in_specs=[pl.BlockSpec(memory_space=pl.ANY)] * 8,
        out_specs=vmem,
        scratch_shapes=[
            pltpu.SMEM((4,), jnp.int32), pltpu.SMEM((8,), jnp.int32),
            pltpu.VMEM((8, 1536), BF16), pltpu.VMEM((8, 1536), BF16), pltpu.VMEM((8, 1536), BF16),
            pltpu.VMEM((4, 1536), BF16), pltpu.VMEM((4, 1536), BF16), pltpu.VMEM((4, 1536), BF16),
            pltpu.VMEM((ROWS_Y, PARTS, 4, HD), BF16),
            pltpu.VMEM((ROWS_Y, 3, 4, HD), BF16),
            pltpu.VMEM((YS, 3, 4, HD), BF16),
            pltpu.VMEM((4, 8, HD), BF16),
            pltpu.VMEM((ZS, 2, YS * PARTS, 4, HD), BF16),
            pltpu.VMEM((512, 2 * HD), BF16),
            pltpu.VMEM((512, 2 * HD), BF16),
            pltpu.VMEM((1024, HD), BF16),
            pltpu.VMEM((1024, 2 * HD), BF16),
            pltpu.VMEM((384, HD), BF16),
            pltpu.VMEM((64, HD), BF16),
            pltpu.VMEM((64, HD), F32),
            pltpu.VMEM((64, 2 * HD), F32),
            pltpu.VMEM((YS, 48, 8, HD), BF16),
            dma((8,)), dma((9,)), dma((12,)), dma((3,)), dma((4,)), dma((3,)), dma((4,)),
            dma((14,)), dma((14,)), dma((16,)), dma((16,)), dma((16,)), dma((12,)),
        ],
        compiler_params=pltpu.CompilerParams(collective_id=0, has_side_effects=True),
        name="coalition_attention",
    )(span_ids, coal_bits, lat_q, lat_k, lat_v, txt_q, txt_k, txt_v)
    return pl.pallas_call(
        laid_out,
        out_shape=(jax.ShapeDtypeStruct((8, 4, 1536), BF16), jax.ShapeDtypeStruct((8, 8, 1536), BF16)),
        in_specs=[vmem],
        out_specs=(pl.BlockSpec(memory_space=pl.ANY),) * 2,
        scratch_shapes=[pltpu.VMEM((8, 4, 1536), BF16), dma((13,))],
        name="laid_out",
    )(pltpu.with_memory_space_constraint(landed, pltpu.VMEM))


def solution(mesh):
    return jax.shard_map(
        per_device,
        mesh=mesh,
        in_specs=(P("seq", None),) * 6 + (P("seq"), P("coal")),
        out_specs=(P("coal", "seq", None), P("coal", "seq", None)),
        check_vma=False,
    )
```

```python
import functools
import math

import jax
import jax.numpy as jnp
from jax import lax
from jax.experimental import pallas as pl
from jax.experimental.pallas import tpu as pltpu
from jax.sharding import PartitionSpec as P

MESH = pl.DeviceIdType.MESH
BF16, F32 = jnp.bfloat16, jnp.float32

YS, XS, ZS = 4, 4, 16
ROWS_Y = 3
HD = 128
SCALE2 = math.log2(math.e) / math.sqrt(HD)
HIDDEN = -1e30
PARTS = 7
FAR = 5
SHIFTS = (FAR, -FAR, 3, -3, 2, -2, 1, -1, 0)


def place():
    seq, coal = lax.axis_index("seq"), lax.axis_index("coal")
    return lax.div(seq, 32), lax.rem(lax.div(seq, 16), 2), lax.rem(seq, 16), lax.div(coal, 2), lax.rem(coal, 2)


def widened(unit):
    return unit.astype(F32)


def kernel(
    spans_in, bits_in, lq_in, lk_in, lv_in, tq_in, tk_in, tv_in, landed,
    spans, bits, lq, lk, lv, tq, tk, tv,
    own, own_q, queries, biases, gathered, text_k, text_v, lat_k, lat_v, bias_rows, base_q, lat_stats, lat_mixed, results,
    in_sem, s_send, s_recv, q_send, q_recv, b_send, b_recv, z_send, z_recv, c_send, c_recv, o_send, o_recv,
):
    y, x_hi, z, x_lo, core = place()
    x = x_hi * 2 + x_lo
    coal = x_lo * 2 + core
    active = y < ROWS_Y

    z_at = {shift: lax.rem(z + shift + ZS, ZS) for shift in (0, 1, 2, 3, FAR, -1, -2, -3, -FAR)}
    column = y * 32 + x_hi * 16

    def at_z(shift):
        return (column + z_at[shift], coal)

    barrier = pltpu.get_barrier_semaphore()

    def greet(partner):
        pl.semaphore_signal(barrier, inc=1, device_id=partner, device_id_type=MESH)

    in_pair = core == x_hi
    step_x = jnp.where(x_lo == 0, XS - 1, 1)
    x_from = jnp.where(in_pair, x, lax.rem(x + step_x, XS))
    coal_from = lax.rem(x_from, 2) * 2 + jnp.where(in_pair, 0, 1)
    pair_from = lax.div(x_from, 2) * 16
    this = column + z
    others = ((this, x_lo * 2 + 1 - core), (this, (1 - x_lo) * 2 + core), (this, (1 - x_lo) * 2 + 1 - core))

    @pl.when(active)
    def _():
        for shift in SHIFTS:
            for y_from in range(YS):
                greet((pair_from + z_at[-shift] + y_from * 32, coal_from))
        for shift in (1, 2, 3):
            greet(at_z(shift))
            greet(at_z(-shift))
        for other in others:
            greet(other)

    for y_from in range(ROWS_Y):
        for x_of in range(XS):
            greet((z + (y_from * 32 + x_of // 2 * 16), x_hi + x_of % 2 * 2))

    loads = [
        pltpu.make_async_copy(src, dst, in_sem.at[n])
        for n, (src, dst) in enumerate(
            ((spans_in, spans), (bits_in, bits), (tk_in, tk), (tv_in, tv), (lk_in, lk), (lv_in, lv), (tq_in, tq), (lq_in, lq))
        )
    ]
    for load in loads:
        load.start()

    for load in loads:
        load.wait()

    sub = lax.broadcasted_iota(jnp.int32, (8, HD), 0)
    lane = lax.broadcasted_iota(jnp.int32, (8, HD), 1)
    upper = sub < 4
    x_to = jnp.where(core == 0, x, lax.rem(x + step_x, XS))
    pair_to = lax.div(x_to, 2) * 16
    coal_to = lax.rem(x_to, 2) * 2 + x_hi
    span = jnp.zeros((8, HD), jnp.int32)
    for row in range(4):
        span = jnp.where(sub == row, spans[row], span)
    one_hot = jnp.where(lane == span, 1.0, 0.0)[:4]
    for y_to in range(ROWS_Y):
        cols = pl.ds(pl.multiple_of((x_to * ROWS_Y + y_to) * HD, HD), HD)
        keys, values, asked = widened(lk[:, cols]), widened(lv[:, cols]), widened(lq[:, cols])
        own[y_to, 0] = tk[:, cols]
        own[y_to, 1] = tv[:, cols]
        own[y_to, 2] = one_hot.astype(BF16)
        for n in range(2):
            own[y_to, 3 + n] = keys[n * 4 : n * 4 + 4].astype(BF16)
            own[y_to, 5 + n] = values[n * 4 : n * 4 + 4].astype(BF16)
            own_q[y_to, 1 + n] = asked[n * 4 : n * 4 + 4].astype(BF16)
        own_q[y_to, 0] = tq[:, cols]
    kept = jnp.zeros((8, HD), jnp.int32)
    for row in range(8):
        kept = jnp.where(sub == row, bits[row], kept)
    shown = jnp.right_shift(kept, jnp.bitwise_and(lane, 15)) & 1
    biases[coal] = jnp.where((lane < 16) & (shown == 0), HIDDEN, 0.0).astype(BF16)
    text_v[:, HD:] = jnp.ones((512, HD), BF16)
    lat_v[:, HD:] = jnp.ones((1024, HD), BF16)

    in_own = (core == 0) & (x_hi == 0) & active
    pl.semaphore_wait(barrier, len(SHIFTS) * ROWS_Y + jnp.where(active, 6 + 3 + 16, 0))

    def remote(src, dst, send, recv, target):
        return pltpu.make_async_remote_copy(
            src_ref=src, dst_ref=dst, send_sem=send, recv_sem=recv, device_id=target, device_id_type=MESH
        )

    def rows_to(n, y_to):
        target = (pair_to + z_at[SHIFTS[n]] + y_to * 32, coal_to)
        there = gathered.at[-SHIFTS[n] % ZS, x_hi, pl.ds(y * PARTS, PARTS)]
        return (own.at[y_to], there, s_send.at[n * ROWS_Y + y_to], s_recv.at[n * YS + y], target)

    def queries_to(y_to):
        target = (pair_to + z + y_to * 32, coal_to)
        return (own_q.at[y_to], queries.at[y], q_send.at[y_to], q_recv.at[y], target)

    def maybe_own(y_to, copy):
        src, dst, send, recv, target = copy
        to_self = in_own & (y == y_to)

        @pl.when(to_self)
        def _():
            pltpu.make_async_copy(src, dst, recv).start()

        @pl.when(jnp.logical_not(to_self))
        def _():
            remote(src, dst, send, recv, target).start()

    for n in range(len(SHIFTS)):
        for y_to in range(ROWS_Y):
            if SHIFTS[n]:
                remote(*rows_to(n, y_to)).start()
            else:
                maybe_own(y_to, rows_to(n, y_to))
                maybe_own(y_to, queries_to(y_to))

    def bias_copies():
        for n, target in enumerate(others):
            yield remote(biases.at[coal], biases.at[coal], b_send.at[n], b_recv.at[coal], target)

    whole = YS * PARTS

    def ring(n, offset, shift, first=0, count=whole):
        here = gathered.at[offset % ZS, core, pl.ds(first, count)]
        there = gathered.at[(offset - shift) % ZS, core, pl.ds(first, count)]
        return remote(here, there, z_send.at[n], z_recv.at[n], at_z(shift))

    def across(offset):
        block = gathered.at[offset % ZS, core]
        return remote(block, block, c_send.at[offset % ZS], c_recv.at[offset % ZS], others[0])

    half = whole // 2
    forwards = [
        (FAR, -3, half, whole - half), (-FAR, 3, 0, half),
        (FAR, -2), (-FAR, 2), (FAR, 1), (FAR, -1), (-FAR, 1), (-FAR, -1),
    ]

    def direct_in(n):
        for y_from in range(YS):
            block = gathered.at[-SHIFTS[n] % ZS, core, pl.ds(y_from * PARTS, PARTS)]
            pltpu.make_async_copy(block, block, s_recv.at[n * YS + y_from]).wait()

    def converted(o):
        for k in range(2):
            part = [[widened(gathered[o, k, n * PARTS + m]) for m in range(PARTS)] for n in range(YS)]

            def rows_of(*which):
                return jnp.concatenate([part[n][m] for n in range(YS) for m in which], axis=0).astype(BF16)

            rows = pl.ds((o * 2 + k) * 16, 16)
            text_k[rows, pl.ds(0, HD)] = rows_of(0)
            text_k[rows, pl.ds(HD, HD)] = rows_of(2)
            text_v[rows, pl.ds(0, HD)] = rows_of(1)
            rows = pl.ds((o * 2 + k) * 32, 32)
            lat_k[rows, :] = rows_of(3, 4)
            lat_v[rows, pl.ds(0, HD)] = rows_of(5, 6)

    nt = (((1,), (1,)), ((), ()))

    @pl.when(active)
    def _():
        for copy in bias_copies():
            copy.start()
        second = [ring(n, *f) for n, f in enumerate(forwards)]
        crossing = [across(o) for o in range(ZS)]
        for n in range(YS):
            pltpu.make_async_copy(queries.at[n], queries.at[n], q_recv.at[n]).wait()
            asked = [widened(queries[n, m]) for m in (0, 0, 1, 2)]
            base_q[pl.ds(n * 16, 16), :] = jnp.concatenate(asked, axis=0).astype(BF16)
        for g in range(4):

            @pl.when(coal != g)
            def _():
                pltpu.make_async_copy(biases.at[g], biases.at[g], b_recv.at[g]).wait()

            unit = widened(biases[g])
            rows = [unit[c : c + 1, :] for c in range(8)]
            parts = [jnp.where(upper, rows[2 * p], rows[2 * p + 1]) for p in range(4)]
            parts += [jnp.broadcast_to(row, (8, HD)) for row in rows]
            bias_rows[pl.ds(g * 96, 96), :] = jnp.concatenate(parts, axis=0).astype(BF16)
        for n in (0, 1):
            direct_in(n)
            for f, copy in zip(forwards, second):
                if f[0] == -SHIFTS[n]:
                    copy.start()
            crossing[-SHIFTS[n] % ZS].start()
        for n in range(2, len(SHIFTS)):
            direct_in(n)
            crossing[-SHIFTS[n] % ZS].start()

        for shift in SHIFTS:
            crossing[-shift % ZS].wait_recv()
            converted(-shift % ZS)
        for n in (4, 5, 6, 7, 2, 3):
            second[n].wait_recv()
            crossing[(forwards[n][0] - forwards[n][1]) % ZS].start()
        second[0].wait_recv()
        second[1].wait_recv()
        crossing[8].start()
        for n in (4, 5, 6, 7, 2, 3, 0):
            o = (forwards[n][0] - forwards[n][1]) % ZS
            crossing[o].wait_recv()
            converted(o)

        scores = lax.dot_general(base_q[...], lat_k[...], nt, preferred_element_type=F32) * SCALE2
        maxima = jnp.max(scores, axis=1, keepdims=True)
        weights = jnp.exp2(scores - maxima).astype(BF16)
        lat_stats[...] = jnp.broadcast_to(maxima, (64, HD))
        lat_mixed[...] = jnp.dot(weights, lat_v[...], preferred_element_type=F32)

        head = x * ROWS_Y + y
        near_last = jnp.where(in_pair, x_lo, jnp.where(x_lo == 0, 1, 0))

        def to_device(row, g):
            target = (((row * 2 + core) * ZS + z), g)
            return (
                (row == y) & (core == x_hi) & (g == coal),
                remote(
                    results.at[row, pl.ds(g * 12, 12)], landed.at[head],
                    o_send.at[row * 4 + g], o_recv.at[head], target,
                ),
            )

        def spread(unit):
            text, latent = unit[:8], unit[8:]
            return jnp.concatenate(([text] * 4 + [latent] * 8) * 4, axis=0)

        def one_row(turn):
            row = lax.rem(y + (2, 1, 3, 0)[turn], YS)
            at_row = pl.ds(pl.multiple_of(row * 16, 16), 16)
            asked = base_q[at_row, :].astype(F32)
            left = spread(asked).astype(BF16)
            full = jnp.concatenate([left, bias_rows[...]], axis=1)
            scores = lax.dot_general(full, text_k[...], nt, preferred_element_type=F32)
            shared = spread(lat_stats[at_row, :])[:, :1]
            maxima = jnp.maximum(jnp.max(scores, axis=1, keepdims=True) * SCALE2, shared)
            weights = jnp.exp2(scores * SCALE2 - maxima).astype(BF16)
            total = jnp.dot(weights, text_v[...], preferred_element_type=F32)
            total = total + jnp.exp2(shared - maxima) * spread(lat_mixed[at_row, :])
            results[row] = (total[:, :HD] / total[:, HD:]).reshape(48, 8, HD).astype(BF16)
            for near in range(4):
                g = lax.rem(2 * near_last + near + 2, 4)
                to_self, copy = to_device(row, g)
                if turn < YS - 1:
                    copy.start()
                    continue

                @pl.when(to_self)
                def _():
                    part = results.at[row, pl.ds(g * 12, 12)]
                    pltpu.make_async_copy(part, landed.at[head], o_recv.at[head]).start()

                @pl.when(jnp.logical_not(to_self))
                def _():
                    copy.start()

        for turn in range(YS):
            one_row(turn)

        for copy in second:
            copy.wait_send()
        for copy in crossing:
            copy.wait_send()
        for copy in bias_copies():
            copy.wait_send()

        def drained(step, _):
            to_self, copy = to_device(lax.div(step, 4), lax.rem(step, 4))

            @pl.when(jnp.logical_not(to_self))
            def _():
                copy.wait_send()

            return 0

        lax.fori_loop(0, 16, drained, 0)

    for n in range(len(SHIFTS)):
        for y_to in range(ROWS_Y):
            if SHIFTS[n]:
                remote(*rows_to(n, y_to)).wait_send()
            else:

                @pl.when(jnp.logical_not(in_own & (y == y_to)))
                def _():
                    remote(*rows_to(n, y_to)).wait_send()
                    remote(*queries_to(y_to)).wait_send()

    for head in range(ROWS_Y * XS):
        pltpu.make_async_copy(landed.at[head], landed.at[head], o_recv.at[head]).wait()


def laid_out(landed, out_t, out_l, text, sems):
    copies = []
    for head in range(ROWS_Y * XS):
        cols = pl.ds(head * HD, HD)
        copies.append(pltpu.make_async_copy(landed.at[head, pl.ds(4, 8)], out_l.at[:, :, cols], sems.at[head]))
        copies[-1].start()
    for head in range(ROWS_Y * XS):
        for pair in range(4):
            unit = widened(landed[head, pair])
            text[2 * pair, :, head * HD : (head + 1) * HD] = unit[:4].astype(BF16)
            text[2 * pair + 1, :, head * HD : (head + 1) * HD] = unit[4:].astype(BF16)
    copies.append(pltpu.make_async_copy(text, out_t, sems.at[12]))
    copies[-1].start()
    for copy in copies:
        copy.wait()


def per_device(lat_q, lat_k, lat_v, txt_q, txt_k, txt_v, span_ids, coal_bits):
    vmem = pl.BlockSpec(memory_space=pltpu.VMEM)
    dma = pltpu.SemaphoreType.DMA
    landed = pl.pallas_call(
        kernel,
        out_shape=pltpu.VMEM((12, 12, 8, HD), BF16),
        in_specs=[pl.BlockSpec(memory_space=pl.ANY)] * 8,
        out_specs=vmem,
        scratch_shapes=[
            pltpu.SMEM((4,), jnp.int32), pltpu.SMEM((8,), jnp.int32),
            pltpu.VMEM((8, 1536), BF16), pltpu.VMEM((8, 1536), BF16), pltpu.VMEM((8, 1536), BF16),
            pltpu.VMEM((4, 1536), BF16), pltpu.VMEM((4, 1536), BF16), pltpu.VMEM((4, 1536), BF16),
            pltpu.VMEM((ROWS_Y, PARTS, 4, HD), BF16),
            pltpu.VMEM((ROWS_Y, 3, 4, HD), BF16),
            pltpu.VMEM((YS, 3, 4, HD), BF16),
            pltpu.VMEM((4, 8, HD), BF16),
            pltpu.VMEM((ZS, 2, YS * PARTS, 4, HD), BF16),
            pltpu.VMEM((512, 2 * HD), BF16),
            pltpu.VMEM((512, 2 * HD), BF16),
            pltpu.VMEM((1024, HD), BF16),
            pltpu.VMEM((1024, 2 * HD), BF16),
            pltpu.VMEM((384, HD), BF16),
            pltpu.VMEM((64, HD), BF16),
            pltpu.VMEM((64, HD), F32),
            pltpu.VMEM((64, 2 * HD), F32),
            pltpu.VMEM((YS, 48, 8, HD), BF16),
            dma((8,)), dma((27,)), dma((36,)), dma((3,)), dma((4,)), dma((3,)), dma((4,)),
            dma((8,)), dma((8,)), dma((16,)), dma((16,)), dma((16,)), dma((12,)),
        ],
        compiler_params=pltpu.CompilerParams(collective_id=0, has_side_effects=True),
        name="coalition_attention",
    )(span_ids, coal_bits, lat_q, lat_k, lat_v, txt_q, txt_k, txt_v)
    return pl.pallas_call(
        laid_out,
        out_shape=(jax.ShapeDtypeStruct((8, 4, 1536), BF16), jax.ShapeDtypeStruct((8, 8, 1536), BF16)),
        in_specs=[vmem],
        out_specs=(pl.BlockSpec(memory_space=pl.ANY),) * 2,
        scratch_shapes=[pltpu.VMEM((8, 4, 1536), BF16), dma((13,))],
        name="laid_out",
    )(pltpu.with_memory_space_constraint(landed, pltpu.VMEM))


def solution(mesh):
    return jax.shard_map(
        per_device,
        mesh=mesh,
        in_specs=(P("seq", None),) * 6 + (P("seq"), P("coal")),
        out_specs=(P("coal", "seq", None), P("coal", "seq", None)),
        check_vma=False,
    )
```
